512 devices in a mesh: band: 8 (over x, z_lo), tm: 64 (over y, z_hi, core).
Axes of the slice: x: 4, y: 8, z: 8 (z_hi: 4, z_lo: 2; z = z_hi * 2 + z_lo), core: 2. Of those that a mesh axis runs over, the one named last changes fastest.
Arguments:
- driven_wave: bfloat16 [2048, 2048], P('tm', 'band'), may hold values from -6 to 6
- responses: bfloat16 [1024, 512, 2048], P('tm', None, 'band'), may hold values from -0.01171875 to 0.01171875
- tap_counts: int32 [2048], P('band'), may hold values from 256 to 1024
- panel_links: int32 [2048, 2], P('band'), may hold values 0 or 1
Outputs:
- far_end: bfloat16 [1024, 2048], P('tm', 'band')
The draws below stay inside these ranges and needn't reach their ends.
All inputs are finite; a program needn't handle non-finite values. No bound on the sum of `panel_links` on one device may be relied on, other than what follows from the above.
Results may differ from the reference program's by a relative error of at most 0.00155.
Values may be sent and summed in bfloat16 or wider, within the bound.
No kernel may reach another device: no remote copies, remote signals or barrier semaphores. Data moves between devices by JAX's collectives and lax.ppermute only.
A program may use at most 64 MiB of HBM per device.

```python
import jax
import jax.numpy as jnp
from jax import lax

GROUP_PORTS = 256
K = 1024
PORTS = 2048
COUPLED = 512
WINDOW = 1024
HISTORY = 2048
N_BAND = 8


def draw_tap_counts(key, part):
    key_values, key_first, key_stride = jax.random.split(key, 3)
    drawn = jax.random.randint(key_values, (PORTS,), K // 4, K + 1, dtype=jnp.int32)
    first_slot = jax.random.randint(key_first, (), 0, PORTS, dtype=jnp.int32)
    stride_draw = jax.random.randint(key_stride, (), 1, PORTS, dtype=jnp.int32)
    second_slot = (first_slot + stride_draw) % PORTS
    return drawn.at[first_slot].set(K).at[second_slot].set(K // 4)


def place_ends(values, stream_key, low, top_value):
    extent = values.shape
    place = [jax.random.randint(jax.random.fold_in(stream_key, axis), (), 0, extent[axis]) for axis in range(len(extent))]
    values = values.at[tuple(place)].set(low)
    longest = extent.index(max(extent))
    place[longest] = (place[longest] + 1) % extent[longest]
    return values.at[tuple(place)].set(top_value)


def block_scale(key, extent, pieces, low, high):
    loudness = 1.0
    for position, parts in pieces:
        draws = jax.random.uniform(jax.random.fold_in(jax.random.fold_in(key, 6), position), (parts,), jnp.float32, low / len(pieces), high / len(pieces))
        loudness = loudness * jnp.repeat(jnp.exp(draws), extent[position] // parts).reshape((-1,) + (1,) * (len(extent) - 1 - position))
    return loudness


def scatter_about(rng, extent, deviation, bound, shards=(), kind=jnp.bfloat16):
    entries = deviation * jax.random.normal(rng, extent, jnp.float32)
    if shards:
        entries = entries * block_scale(rng, extent, shards, -0.22, 0.18)
    return jnp.clip(entries, -bound, bound).astype(kind)


def setup_inputs(seed: int = 0) -> dict:
    keys = jax.random.split(jax.random.key(seed), 5)
    driven_wave = scatter_about(keys[0], (HISTORY, PORTS), 1.0, 6.0, ((0, 64), (1, 8)))
    responses = scatter_about(keys[1], (K, COUPLED, PORTS), (K * GROUP_PORTS) ** -0.5, 0.01171875, ((0, 64), (2, 8)))
    tap_counts = draw_tap_counts(jax.random.fold_in(keys[4], 71), 0)
    panel_links = place_ends((jax.random.randint(keys[3], (PORTS, 2), 0, 4) < 3).astype(jnp.int32), jax.random.fold_in(keys[3], 1), 0, 1)
    return dict(driven_wave=driven_wave, responses=responses, tap_counts=tap_counts, panel_links=panel_links)


def reference(driven_wave, responses, tap_counts, panel_links):
    group_ports = GROUP_PORTS
    half_width = group_ports // 2
    padded = jnp.pad(driven_wave, ((0, 0), (half_width, half_width)))
    coupled = jnp.stack([padded[:, band_index * group_ports: band_index * group_ports + 2 * group_ports] for band_index in range(N_BAND)], axis=1)
    port_index = jnp.arange(COUPLED, dtype=jnp.int32)[:, None]
    lower_open = panel_links[None, :, 0] == 1
    upper_open = panel_links[None, :, 1] == 1
    couple_open = jnp.where(port_index < half_width, lower_open, jnp.where(port_index >= half_width + group_ports, upper_open, True))

    def accumulate(block_index, running):
        lead_tap = (8 * block_index).astype(jnp.int32)
        tap_block = lax.dynamic_slice_in_dim(responses, lead_tap, 8, 0)
        tap_index = lead_tap + jnp.arange(8, dtype=jnp.int32)
        keep_mask = (tap_index[:, None] < tap_counts[None, :])[:, None, :] & couple_open[None, :, :]
        tap_block = jnp.where(keep_mask, tap_block, jnp.zeros_like(tap_block)).astype(jnp.float32)
        tap_block = tap_block.reshape(8, COUPLED, N_BAND, group_ports)
        window = lax.dynamic_slice_in_dim(coupled, (K - lead_tap - 7).astype(jnp.int32), WINDOW + 7, 0)
        stacked = jnp.stack([window[7 - shift_index: 7 - shift_index + WINDOW] for shift_index in range(8)], axis=0).astype(jnp.float32)
        return running + jnp.einsum("ktgq,kqgp->tgp", stacked, tap_block, precision=lax.Precision.HIGHEST)

    running = lax.fori_loop(0, K // 8, accumulate, jnp.zeros((WINDOW, N_BAND, group_ports), jnp.float32))
    return running.reshape(WINDOW, PORTS).astype(jnp.bfloat16)
```

```python
import jax
import jax.numpy as jnp
from jax import lax
from jax.sharding import Mesh
from jax.sharding import PartitionSpec as P

TM = ("y", "zh", "core")


def extended(cells, width):
    count = lax.axis_size("band")
    ends = count - 1
    head = cells[:, :width]
    tail = cells[:, cells.shape[1] - width :]
    return jnp.concatenate(
        [
            lax.ppermute(tail, "band", [(i, (i + 1) % count) for i in range(ends)]),
            cells,
            lax.ppermute(head, "band", [((i + 1) % count, i) for i in range(ends)]),
        ],
        axis=1,
    )


def masked_weights(responses, tap_counts, panel_links, first_tap):
    tap_dev, coupled_ports, group_ports = responses.shape
    half_width = (coupled_ports - group_ports) // 2
    tap_index = first_tap + jnp.arange(tap_dev, dtype=jnp.int32)
    tap_alive = tap_index[:, None] < tap_counts[None, :]
    port_index = jnp.arange(coupled_ports, dtype=jnp.int32)[:, None]
    lower_open = panel_links[None, :, 0] == 1
    upper_open = panel_links[None, :, 1] == 1
    couple_open = jnp.where(
        port_index < half_width,
        lower_open,
        jnp.where(port_index >= half_width + group_ports, upper_open, True),
    )
    keep_mask = tap_alive[:, None, :] & couple_open[None, :, :]
    return jnp.where(keep_mask, responses, jnp.zeros_like(responses))


def gather_history(x):
    x = lax.all_gather(x, "core", axis=0, tiled=True)
    x = lax.all_gather(x, "zh", axis=0, tiled=True)
    return lax.all_gather(x, "y", axis=0, tiled=True)


def tm_index():
    return (lax.axis_index("y") * lax.axis_size("zh") + lax.axis_index("zh")) * lax.axis_size(
        "core"
    ) + lax.axis_index("core")


def per_device(driven_wave, responses, tap_counts, panel_links):
    tap_dev = responses.shape[0]
    group_ports = driven_wave.shape[1]
    half_width = group_ports // 2
    n_tm = lax.axis_size("y") * lax.axis_size("zh") * lax.axis_size("core")
    total_taps = tap_dev * n_tm
    window_len = driven_wave.shape[0] * n_tm - total_taps
    me = tm_index()
    first_tap = me * tap_dev
    weights = masked_weights(responses, tap_counts, panel_links, first_tap)[::-1]
    history = gather_history(extended(driven_wave, half_width))
    base = total_taps - first_tap - (tap_dev - 1)
    window = lax.dynamic_slice_in_dim(history, base, window_len + tap_dev - 1, 0)
    partial = lax.conv_general_dilated(
        window[None],
        weights,
        window_strides=(1,),
        padding="VALID",
        dimension_numbers=("NWC", "WIO", "NWC"),
        preferred_element_type=jnp.float32,
    )[0]
    blocks = partial.reshape(n_tm, window_len // n_tm, group_ports)
    summed = lax.all_to_all(blocks, TM, 0, 0, tiled=True).sum(0)
    return summed.astype(jnp.bfloat16)


def solution(mesh):
    band, tm = mesh.devices.shape
    view = Mesh(mesh.devices.reshape(band, tm // 8, 4, 2), ("band",) + TM)
    return jax.shard_map(
        per_device,
        mesh=view,
        in_specs=(P(TM, "band"), P(TM, None, "band"), P("band"), P("band", None)),
        out_specs=P(TM, "band"),
        check_vma=False,
    )
```

```python
import jax
import jax.numpy as jnp
from jax import lax
from jax.sharding import Mesh
from jax.sharding import PartitionSpec as P

TM = ("y", "zh", "core")


def extended(cells, width):
    count = lax.axis_size("band")
    ends = count - 1
    head = cells[:, :width]
    tail = cells[:, cells.shape[1] - width :]
    return jnp.concatenate(
        [
            lax.ppermute(tail, "band", [(i, (i + 1) % count) for i in range(ends)]),
            cells,
            lax.ppermute(head, "band", [((i + 1) % count, i) for i in range(ends)]),
        ],
        axis=1,
    )


def masked_weights(responses, tap_counts, panel_links, first_tap):
    tap_dev, coupled_ports, group_ports = responses.shape
    half_width = (coupled_ports - group_ports) // 2
    tap_index = first_tap + jnp.arange(tap_dev, dtype=jnp.int32)
    tap_alive = tap_index[:, None] < tap_counts[None, :]
    port_index = jnp.arange(coupled_ports, dtype=jnp.int32)[:, None]
    lower_open = panel_links[None, :, 0] == 1
    upper_open = panel_links[None, :, 1] == 1
    couple_open = jnp.where(
        port_index < half_width,
        lower_open,
        jnp.where(port_index >= half_width + group_ports, upper_open, True),
    )
    keep_mask = tap_alive[:, None, :] & couple_open[None, :, :]
    return jnp.where(keep_mask, responses, jnp.zeros_like(responses))


def swap_core(x):
    return lax.ppermute(x, "core", [(0, 1), (1, 0)])


def gather_history(x):
    chips = lax.axis_size("y") * lax.axis_size("zh")
    spread = jnp.broadcast_to(x[None], (chips,) + x.shape)
    mine = lax.all_to_all(spread, ("y", "zh"), 0, 0, tiled=True)
    other = swap_core(mine)
    first = lax.axis_index("core") == 0
    pair = jnp.stack([jnp.where(first, mine, other), jnp.where(first, other, mine)], 1)
    return pair.reshape(-1, x.shape[1])


def reduce_scatter(partial, n_tm):
    chips = n_tm // 2
    blocks = partial.reshape(chips, 2, partial.shape[0] // n_tm, partial.shape[1])
    first = lax.axis_index("core") == 0
    keep = jnp.where(first, blocks[:, 0], blocks[:, 1])
    give = jnp.where(first, blocks[:, 1], blocks[:, 0])
    combined = keep + swap_core(give)
    return lax.all_to_all(combined, ("y", "zh"), 0, 0, tiled=True).sum(0)


def tm_index():
    return (lax.axis_index("y") * lax.axis_size("zh") + lax.axis_index("zh")) * lax.axis_size(
        "core"
    ) + lax.axis_index("core")


def per_device(driven_wave, responses, tap_counts, panel_links):
    tap_dev = responses.shape[0]
    group_ports = driven_wave.shape[1]
    half_width = group_ports // 2
    n_tm = lax.axis_size("y") * lax.axis_size("zh") * lax.axis_size("core")
    total_taps = tap_dev * n_tm
    window_len = driven_wave.shape[0] * n_tm - total_taps
    me = tm_index()
    first_tap = me * tap_dev
    weights = masked_weights(responses, tap_counts, panel_links, first_tap)[::-1]
    history = gather_history(extended(driven_wave, half_width))
    base = total_taps - first_tap - (tap_dev - 1)
    window = lax.dynamic_slice_in_dim(history, base, window_len + tap_dev - 1, 0)
    partial = lax.conv_general_dilated(
        window[None],
        weights,
        window_strides=(1,),
        padding="VALID",
        dimension_numbers=("NWC", "WIO", "NWC"),
        preferred_element_type=jnp.float32,
    )[0]
    summed = reduce_scatter(partial, n_tm)
    return summed.astype(jnp.bfloat16)


def solution(mesh):
    band, tm = mesh.devices.shape
    view = Mesh(mesh.devices.reshape(band, tm // 8, 4, 2), ("band",) + TM)
    return jax.shard_map(
        per_device,
        mesh=view,
        in_specs=(P(TM, "band"), P(TM, None, "band"), P("band"), P("band", None)),
        out_specs=P(TM, "band"),
        check_vma=False,
    )
```

```python
import jax
import jax.numpy as jnp
from jax import lax
from jax.experimental import pallas as pl
from jax.experimental.pallas import tpu as pltpu
from jax.sharding import Mesh
from jax.sharding import PartitionSpec as P

TM = ("y", "zh", "core")


def extended(cells, width):
    count = lax.axis_size("band")
    ends = count - 1
    head = cells[:, :width]
    tail = cells[:, cells.shape[1] - width :]
    return jnp.concatenate(
        [
            lax.ppermute(tail, "band", [(i, (i + 1) % count) for i in range(ends)]),
            cells,
            lax.ppermute(head, "band", [((i + 1) % count, i) for i in range(ends)]),
        ],
        axis=1,
    )


def masked_weights(responses, tap_counts, panel_links, first_tap):
    tap_dev, coupled_ports, group_ports = responses.shape
    half_width = (coupled_ports - group_ports) // 2
    tap_index = first_tap + jnp.arange(tap_dev, dtype=jnp.int32)
    tap_alive = tap_index[:, None] < tap_counts[None, :]
    port_index = jnp.arange(coupled_ports, dtype=jnp.int32)[:, None]
    lower_open = panel_links[None, :, 0] == 1
    upper_open = panel_links[None, :, 1] == 1
    couple_open = jnp.where(
        port_index < half_width,
        lower_open,
        jnp.where(port_index >= half_width + group_ports, upper_open, True),
    )
    keep_mask = tap_alive[:, None, :] & couple_open[None, :, :]
    return jnp.where(keep_mask, responses, jnp.zeros_like(responses))


def swap_core(x):
    return lax.ppermute(x, "core", [(0, 1), (1, 0)])


def gather_history(x):
    chips = lax.axis_size("y") * lax.axis_size("zh")
    spread = jnp.broadcast_to(x[None], (chips,) + x.shape)
    mine = lax.all_to_all(spread, ("y", "zh"), 0, 0, tiled=True)
    other = swap_core(mine)
    first = lax.axis_index("core") == 0
    pair = jnp.stack([jnp.where(first, mine, other), jnp.where(first, other, mine)], 1)
    return pair.reshape(-1, x.shape[1])


def reduce_scatter(partial, n_tm):
    chips = n_tm // 2
    blocks = partial.reshape(chips, 2, partial.shape[0] // n_tm, partial.shape[1])
    first = lax.axis_index("core") == 0
    keep = jnp.where(first, blocks[:, 0], blocks[:, 1])
    give = jnp.where(first, blocks[:, 1], blocks[:, 0])
    combined = keep + swap_core(give)
    return lax.all_to_all(combined, ("y", "zh"), 0, 0, tiled=True).sum(0)


def tm_index():
    return (lax.axis_index("y") * lax.axis_size("zh") + lax.axis_index("zh")) * lax.axis_size(
        "core"
    ) + lax.axis_index("core")


ROW_TILE = 256


def conv_kernel(x_ref, w_ref, m_ref, o_ref, wm_ref):
    taps, coupled, ports = w_ref.shape
    half = (coupled - ports) // 2
    for k in range(taps):
        marks = m_ref[k]
        for lo, hi, row in ((0, half, 0), (half, half + ports, 1), (half + ports, coupled, 2)):
            keep = marks[row : row + 1, :] != 0
            block = w_ref[k, lo:hi, :]
            wm_ref[k, lo:hi, :] = jnp.where(keep, block, jnp.zeros_like(block))
    rows = o_ref.shape[0]
    for r in range(rows // ROW_TILE):
        start = r * ROW_TILE
        acc = jnp.zeros((ROW_TILE, ports), jnp.float32)
        for k in range(taps):
            shift = taps - k
            acc = acc + jnp.dot(
                x_ref[start + shift : start + shift + ROW_TILE, :],
                wm_ref[k],
                preferred_element_type=jnp.float32,
            )
        o_ref[start : start + ROW_TILE, :] = acc


def masked_conv(window, responses, marks, rows):
    taps, coupled, ports = responses.shape
    vmem = pl.BlockSpec(memory_space=pltpu.VMEM)
    return pl.pallas_call(
        conv_kernel,
        out_shape=jax.ShapeDtypeStruct((rows, ports), jnp.float32),
        in_specs=[vmem, vmem, vmem],
        out_specs=vmem,
        scratch_shapes=[pltpu.VMEM((taps, coupled, ports), responses.dtype)],
        compiler_params=pltpu.CompilerParams(vmem_limit_bytes=48 * 1024 * 1024),
        cost_estimate=pl.CostEstimate(
            flops=2 * rows * taps * coupled * ports,
            transcendentals=0,
            bytes_accessed=window.size * 2 + responses.size * 2 + rows * ports * 4,
        ),
    )(window, responses, marks)


def tap_marks(tap_counts, panel_links, first_tap, taps):
    tap_index = first_tap + jnp.arange(taps, dtype=jnp.int32)
    alive = tap_index[:, None] < tap_counts[None, :]
    lower = alive & (panel_links[None, :, 0] == 1)
    upper = alive & (panel_links[None, :, 1] == 1)
    marks = jnp.stack([lower, alive, upper], 1).astype(jnp.int32)
    return jnp.pad(marks, ((0, 0), (0, 5), (0, 0)))


def per_device(driven_wave, responses, tap_counts, panel_links):
    tap_dev = responses.shape[0]
    group_ports = driven_wave.shape[1]
    half_width = group_ports // 2
    n_tm = lax.axis_size("y") * lax.axis_size("zh") * lax.axis_size("core")
    total_taps = tap_dev * n_tm
    window_len = driven_wave.shape[0] * n_tm - total_taps
    me = tm_index()
    first_tap = me * tap_dev
    history = gather_history(extended(driven_wave, half_width))
    base = total_taps - first_tap - tap_dev
    window = lax.dynamic_slice_in_dim(history, base, window_len + tap_dev, 0)
    marks = tap_marks(tap_counts, panel_links, first_tap, tap_dev)
    partial = masked_conv(window, responses, marks, window_len)
    summed = reduce_scatter(partial, n_tm)
    return summed.astype(jnp.bfloat16)


def solution(mesh):
    band, tm = mesh.devices.shape
    view = Mesh(mesh.devices.reshape(band, tm // 8, 4, 2), ("band",) + TM)
    return jax.shard_map(
        per_device,
        mesh=view,
        in_specs=(P(TM, "band"), P(TM, None, "band"), P("band"), P("band", None)),
        out_specs=P(TM, "band"),
        check_vma=False,
    )
```

```python
import jax
import jax.numpy as jnp
from jax import lax
from jax.experimental import pallas as pl
from jax.experimental.pallas import tpu as pltpu
from jax.sharding import Mesh
from jax.sharding import PartitionSpec as P

TM = ("y", "zh", "core")


def extended(cells, width):
    count = lax.axis_size("band")
    ends = count - 1
    head = cells[:, :width]
    tail = cells[:, cells.shape[1] - width :]
    return jnp.concatenate(
        [
            lax.ppermute(tail, "band", [(i, (i + 1) % count) for i in range(ends)]),
            cells,
            lax.ppermute(head, "band", [((i + 1) % count, i) for i in range(ends)]),
        ],
        axis=1,
    )


def masked_weights(responses, tap_counts, panel_links, first_tap):
    tap_dev, coupled_ports, group_ports = responses.shape
    half_width = (coupled_ports - group_ports) // 2
    tap_index = first_tap + jnp.arange(tap_dev, dtype=jnp.int32)
    tap_alive = tap_index[:, None] < tap_counts[None, :]
    port_index = jnp.arange(coupled_ports, dtype=jnp.int32)[:, None]
    lower_open = panel_links[None, :, 0] == 1
    upper_open = panel_links[None, :, 1] == 1
    couple_open = jnp.where(
        port_index < half_width,
        lower_open,
        jnp.where(port_index >= half_width + group_ports, upper_open, True),
    )
    keep_mask = tap_alive[:, None, :] & couple_open[None, :, :]
    return jnp.where(keep_mask, responses, jnp.zeros_like(responses))


def swap_core(x):
    return lax.ppermute(x, "core", [(0, 1), (1, 0)])


def gather_own(x):
    chips = lax.axis_size("y") * lax.axis_size("zh")
    spread = jnp.broadcast_to(x[None], (chips,) + x.shape)
    mine = lax.all_to_all(spread, ("y", "zh"), 0, 0, tiled=True)
    other = swap_core(mine)
    first = lax.axis_index("core") == 0
    pair = jnp.stack([jnp.where(first, mine, other), jnp.where(first, other, mine)], 1)
    return pair.reshape(-1, x.shape[1])


def halo_columns(cells, width):
    count = lax.axis_size("band")
    ends = count - 1
    head = cells[:, :width]
    tail = cells[:, cells.shape[1] - width :]
    below = lax.ppermute(tail, "band", [(i, (i + 1) % count) for i in range(ends)])
    above = lax.ppermute(head, "band", [((i + 1) % count, i) for i in range(ends)])
    return jnp.concatenate([below, above], axis=1)


def reduce_scatter(partial, n_tm):
    chips = n_tm // 2
    blocks = partial.reshape(chips, 2, partial.shape[0] // n_tm, partial.shape[1])
    first = lax.axis_index("core") == 0
    keep = jnp.where(first, blocks[:, 0], blocks[:, 1])
    give = jnp.where(first, blocks[:, 1], blocks[:, 0])
    combined = keep + swap_core(give)
    return lax.all_to_all(combined, ("y", "zh"), 0, 0, tiled=True).sum(0)


def tm_index():
    return (lax.axis_index("y") * lax.axis_size("zh") + lax.axis_index("zh")) * lax.axis_size(
        "core"
    ) + lax.axis_index("core")


ROW_TILE = 256


def conv_kernel(xo_ref, xh_ref, w_ref, m_ref, o_ref, wo_ref, wh_ref):
    taps, coupled, ports = w_ref.shape
    half = (coupled - ports) // 2
    for k in range(taps):
        marks = m_ref[k]
        for lo, hi, row, dst, at in (
            (0, half, 0, wh_ref, 0),
            (half, half + ports, 1, wo_ref, 0),
            (half + ports, coupled, 2, wh_ref, half),
        ):
            keep = marks[row : row + 1, :] != 0
            block = w_ref[k, lo:hi, :]
            dst[k, at : at + hi - lo, :] = jnp.where(keep, block, jnp.zeros_like(block))
    rows = o_ref.shape[0]
    for r in range(rows // ROW_TILE):
        start = r * ROW_TILE
        acc = jnp.zeros((ROW_TILE, ports), jnp.float32)
        for k in range(taps):
            shift = taps - k
            acc = acc + jnp.dot(
                xo_ref[start + shift : start + shift + ROW_TILE, :],
                wo_ref[k],
                preferred_element_type=jnp.float32,
            )
            acc = acc + jnp.dot(
                xh_ref[start + shift : start + shift + ROW_TILE, :],
                wh_ref[k],
                preferred_element_type=jnp.float32,
            )
        o_ref[start : start + ROW_TILE, :] = acc


def masked_conv(own, halo, responses, marks, rows):
    taps, coupled, ports = responses.shape
    vmem = pl.BlockSpec(memory_space=pltpu.VMEM)
    return pl.pallas_call(
        conv_kernel,
        out_shape=jax.ShapeDtypeStruct((rows, ports), jnp.float32),
        in_specs=[vmem, vmem, vmem, vmem],
        out_specs=vmem,
        scratch_shapes=[
            pltpu.VMEM((taps, ports, ports), responses.dtype),
            pltpu.VMEM((taps, coupled - ports, ports), responses.dtype),
        ],
        compiler_params=pltpu.CompilerParams(vmem_limit_bytes=48 * 1024 * 1024),
        cost_estimate=pl.CostEstimate(
            flops=2 * rows * taps * coupled * ports,
            transcendentals=0,
            bytes_accessed=(own.size + halo.size) * 2 + responses.size * 2 + rows * ports * 4,
        ),
    )(own, halo, responses, marks)


def tap_marks(tap_counts, panel_links, first_tap, taps):
    tap_index = first_tap + jnp.arange(taps, dtype=jnp.int32)
    alive = tap_index[:, None] < tap_counts[None, :]
    lower = alive & (panel_links[None, :, 0] == 1)
    upper = alive & (panel_links[None, :, 1] == 1)
    marks = jnp.stack([lower, alive, upper], 1).astype(jnp.int32)
    return jnp.pad(marks, ((0, 0), (0, 5), (0, 0)))


def per_device(driven_wave, responses, tap_counts, panel_links):
    tap_dev = responses.shape[0]
    group_ports = driven_wave.shape[1]
    half_width = group_ports // 2
    n_tm = lax.axis_size("y") * lax.axis_size("zh") * lax.axis_size("core")
    total_taps = tap_dev * n_tm
    window_len = driven_wave.shape[0] * n_tm - total_taps
    me = tm_index()
    first_tap = me * tap_dev
    halo = lax.all_gather(halo_columns(driven_wave, half_width), TM, axis=0, tiled=True)
    own = gather_own(driven_wave)
    base = total_taps - first_tap - tap_dev
    own_window = lax.dynamic_slice_in_dim(own, base, window_len + tap_dev, 0)
    halo_window = lax.dynamic_slice_in_dim(halo, base, window_len + tap_dev, 0)
    marks = tap_marks(tap_counts, panel_links, first_tap, tap_dev)
    partial = masked_conv(own_window, halo_window, responses, marks, window_len)
    summed = reduce_scatter(partial, n_tm)
    return summed.astype(jnp.bfloat16)


def solution(mesh):
    band, tm = mesh.devices.shape
    view = Mesh(mesh.devices.reshape(band, tm // 8, 4, 2), ("band",) + TM)
    return jax.shard_map(
        per_device,
        mesh=view,
        in_specs=(P(TM, "band"), P(TM, None, "band"), P("band"), P("band", None)),
        out_specs=P(TM, "band"),
        check_vma=False,
    )
```

```python
import jax
import jax.numpy as jnp
from jax import lax
from jax.experimental import pallas as pl
from jax.experimental.pallas import tpu as pltpu
from jax.sharding import Mesh
from jax.sharding import PartitionSpec as P

TM = ("y", "zh", "core")


def extended(cells, width):
    count = lax.axis_size("band")
    ends = count - 1
    head = cells[:, :width]
    tail = cells[:, cells.shape[1] - width :]
    return jnp.concatenate(
        [
            lax.ppermute(tail, "band", [(i, (i + 1) % count) for i in range(ends)]),
            cells,
            lax.ppermute(head, "band", [((i + 1) % count, i) for i in range(ends)]),
        ],
        axis=1,
    )


def masked_weights(responses, tap_counts, panel_links, first_tap):
    tap_dev, coupled_ports, group_ports = responses.shape
    half_width = (coupled_ports - group_ports) // 2
    tap_index = first_tap + jnp.arange(tap_dev, dtype=jnp.int32)
    tap_alive = tap_index[:, None] < tap_counts[None, :]
    port_index = jnp.arange(coupled_ports, dtype=jnp.int32)[:, None]
    lower_open = panel_links[None, :, 0] == 1
    upper_open = panel_links[None, :, 1] == 1
    couple_open = jnp.where(
        port_index < half_width,
        lower_open,
        jnp.where(port_index >= half_width + group_ports, upper_open, True),
    )
    keep_mask = tap_alive[:, None, :] & couple_open[None, :, :]
    return jnp.where(keep_mask, responses, jnp.zeros_like(responses))


def swap_core(x):
    return lax.ppermute(x, "core", [(0, 1), (1, 0)])


def gather_own(x):
    chips = lax.axis_size("y") * lax.axis_size("zh")
    spread = jnp.broadcast_to(x[None], (chips,) + x.shape)
    mine = lax.all_to_all(spread, ("y", "zh"), 0, 0, tiled=True)
    other = swap_core(mine)
    first = lax.axis_index("core") == 0
    pair = jnp.stack([jnp.where(first, mine, other), jnp.where(first, other, mine)], 1)
    return pair.reshape(-1, x.shape[1])


def halo_columns(cells, width):
    count = lax.axis_size("band")
    ends = count - 1
    head = cells[:, :width]
    tail = cells[:, cells.shape[1] - width :]
    below = lax.ppermute(tail, "band", [(i, (i + 1) % count) for i in range(ends)])
    above = lax.ppermute(head, "band", [((i + 1) % count, i) for i in range(ends)])
    return jnp.concatenate([below, above], axis=1)


def reduce_scatter(partial, n_tm):
    chips = n_tm // 2
    blocks = partial.reshape(chips, 2, partial.shape[0] // n_tm, partial.shape[1])
    first = lax.axis_index("core") == 0
    keep = jnp.where(first, blocks[:, 0], blocks[:, 1])
    give = jnp.where(first, blocks[:, 1], blocks[:, 0])
    combined = keep + swap_core(give)
    return lax.all_to_all(combined, ("y", "zh"), 0, 0, tiled=True).sum(0)


def tm_index():
    return (lax.axis_index("y") * lax.axis_size("zh") + lax.axis_index("zh")) * lax.axis_size(
        "core"
    ) + lax.axis_index("core")


ROW_TILE = 256


def conv_kernel(xo_ref, xh_ref, w_ref, m_ref, o_ref, wo_ref, wh_ref):
    taps, coupled, ports = w_ref.shape
    half = (coupled - ports) // 2
    for k in range(taps):
        marks = m_ref[k]
        for lo, hi, row, dst, at in (
            (0, half, 0, wh_ref, 0),
            (half, half + ports, 1, wo_ref, 0),
            (half + ports, coupled, 2, wh_ref, half),
        ):
            keep = marks[row : row + 1, :] != 0
            block = w_ref[k, lo:hi, :]
            dst[k, at : at + hi - lo, :] = jnp.where(keep, block, jnp.zeros_like(block))
    rows = o_ref.shape[0]
    for r in range(rows // ROW_TILE):
        start = r * ROW_TILE
        acc = jnp.zeros((ROW_TILE, ports), jnp.float32)
        for k in range(taps):
            shift = taps - k
            acc = acc + jnp.dot(
                xo_ref[start + shift : start + shift + ROW_TILE, :],
                wo_ref[k],
                preferred_element_type=jnp.float32,
            )
            acc = acc + jnp.dot(
                xh_ref[start + shift : start + shift + ROW_TILE, :],
                wh_ref[k],
                preferred_element_type=jnp.float32,
            )
        o_ref[start : start + ROW_TILE, :] = acc


def masked_conv(own, halo, responses, marks, rows):
    taps, coupled, ports = responses.shape
    vmem = pl.BlockSpec(memory_space=pltpu.VMEM)
    return pl.pallas_call(
        conv_kernel,
        out_shape=jax.ShapeDtypeStruct((rows, ports), jnp.float32),
        in_specs=[vmem, vmem, vmem, vmem],
        out_specs=vmem,
        scratch_shapes=[
            pltpu.VMEM((taps, ports, ports), responses.dtype),
            pltpu.VMEM((taps, coupled - ports, ports), responses.dtype),
        ],
        compiler_params=pltpu.CompilerParams(vmem_limit_bytes=48 * 1024 * 1024),
        cost_estimate=pl.CostEstimate(
            flops=2 * rows * taps * coupled * ports,
            transcendentals=0,
            bytes_accessed=(own.size + halo.size) * 2 + responses.size * 2 + rows * ports * 4,
        ),
    )(own, halo, responses, marks)


def tap_marks(tap_counts, panel_links, first_tap, taps):
    tap_index = first_tap + jnp.arange(taps, dtype=jnp.int32)
    alive = tap_index[:, None] < tap_counts[None, :]
    lower = alive & (panel_links[None, :, 0] == 1)
    upper = alive & (panel_links[None, :, 1] == 1)
    marks = jnp.stack([lower, alive, upper], 1).astype(jnp.int32)
    return jnp.pad(marks, ((0, 0), (0, 5), (0, 0)))


def per_device(driven_wave, responses, tap_counts, panel_links):
    tap_dev = responses.shape[0]
    group_ports = driven_wave.shape[1]
    half_width = group_ports // 2
    n_tm = lax.axis_size("y") * lax.axis_size("zh") * lax.axis_size("core")
    total_taps = tap_dev * n_tm
    window_len = driven_wave.shape[0] * n_tm - total_taps
    me = tm_index()
    first_tap = me * tap_dev
    own = gather_own(driven_wave)
    halo = gather_own(halo_columns(driven_wave, half_width))
    base = total_taps - first_tap - tap_dev
    own_window = lax.dynamic_slice_in_dim(own, base, window_len + tap_dev, 0)
    halo_window = lax.dynamic_slice_in_dim(halo, base, window_len + tap_dev, 0)
    marks = tap_marks(tap_counts, panel_links, first_tap, tap_dev)
    partial = masked_conv(own_window, halo_window, responses, marks, window_len)
    summed = reduce_scatter(partial, n_tm)
    return summed.astype(jnp.bfloat16)


def solution(mesh):
    band, tm = mesh.devices.shape
    view = Mesh(mesh.devices.reshape(band, tm // 8, 4, 2), ("band",) + TM)
    return jax.shard_map(
        per_device,
        mesh=view,
        in_specs=(P(TM, "band"), P(TM, None, "band"), P("band"), P("band", None)),
        out_specs=P(TM, "band"),
        check_vma=False,
    )
```

```python
import jax
import jax.numpy as jnp
from jax import lax
from jax.experimental import pallas as pl
from jax.experimental.pallas import tpu as pltpu
from jax.sharding import Mesh
from jax.sharding import PartitionSpec as P

TM = ("y", "zh", "core")


def extended(cells, width):
    count = lax.axis_size("band")
    ends = count - 1
    head = cells[:, :width]
    tail = cells[:, cells.shape[1] - width :]
    return jnp.concatenate(
        [
            lax.ppermute(tail, "band", [(i, (i + 1) % count) for i in range(ends)]),
            cells,
            lax.ppermute(head, "band", [((i + 1) % count, i) for i in range(ends)]),
        ],
        axis=1,
    )


def masked_weights(responses, tap_counts, panel_links, first_tap):
    tap_dev, coupled_ports, group_ports = responses.shape
    half_width = (coupled_ports - group_ports) // 2
    tap_index = first_tap + jnp.arange(tap_dev, dtype=jnp.int32)
    tap_alive = tap_index[:, None] < tap_counts[None, :]
    port_index = jnp.arange(coupled_ports, dtype=jnp.int32)[:, None]
    lower_open = panel_links[None, :, 0] == 1
    upper_open = panel_links[None, :, 1] == 1
    couple_open = jnp.where(
        port_index < half_width,
        lower_open,
        jnp.where(port_index >= half_width + group_ports, upper_open, True),
    )
    keep_mask = tap_alive[:, None, :] & couple_open[None, :, :]
    return jnp.where(keep_mask, responses, jnp.zeros_like(responses))


def swap_core(x):
    return lax.ppermute(x, "core", [(0, 1), (1, 0)])


def gather_history(x):
    chips = lax.axis_size("y") * lax.axis_size("zh")
    spread = jnp.broadcast_to(x[None], (chips,) + x.shape)
    mine = lax.all_to_all(spread, ("y", "zh"), 0, 0, tiled=True)
    other = swap_core(mine)
    first = lax.axis_index("core") == 0
    pair = jnp.stack([jnp.where(first, mine, other), jnp.where(first, other, mine)], 1)
    return pair.reshape(-1, x.shape[1])


def reduce_scatter(partial, n_tm):
    chips = n_tm // 2
    blocks = partial.reshape(chips, 2, partial.shape[0] // n_tm, partial.shape[1])
    first = lax.axis_index("core") == 0
    keep = jnp.where(first, blocks[:, 0], blocks[:, 1])
    give = jnp.where(first, blocks[:, 1], blocks[:, 0])
    combined = keep + swap_core(give)
    return lax.all_to_all(combined, ("y", "zh"), 0, 0, tiled=True).sum(0)


def tm_index():
    return (lax.axis_index("y") * lax.axis_size("zh") + lax.axis_index("zh")) * lax.axis_size(
        "core"
    ) + lax.axis_index("core")


ROW_TILE = 256


def mask_kernel(w_ref, m_ref, wm_ref):
    taps, coupled, ports = w_ref.shape
    half = (coupled - ports) // 2
    for k in range(taps):
        marks = m_ref[k]
        for lo, hi, row in ((0, half, 0), (half, half + ports, 1), (half + ports, coupled, 2)):
            keep = marks[row : row + 1, :] != 0
            block = w_ref[k, lo:hi, :]
            wm_ref[k, lo:hi, :] = jnp.where(keep, block, jnp.zeros_like(block))


def masked_weights_kernel(responses, marks):
    vmem = pl.BlockSpec(memory_space=pltpu.VMEM)
    return pl.pallas_call(
        mask_kernel,
        out_shape=jax.ShapeDtypeStruct(responses.shape, responses.dtype),
        in_specs=[vmem, vmem],
        out_specs=vmem,
        compiler_params=pltpu.CompilerParams(vmem_limit_bytes=48 * 1024 * 1024),
        cost_estimate=pl.CostEstimate(
            flops=0, transcendentals=0, bytes_accessed=responses.size * 4
        ),
    )(responses, marks)


def conv_kernel(x_ref, wm_ref, o_ref):
    taps, coupled, ports = wm_ref.shape
    rows = o_ref.shape[0]
    for r in range(rows // ROW_TILE):
        start = r * ROW_TILE
        acc = jnp.zeros((ROW_TILE, ports), jnp.float32)
        for k in range(taps):
            shift = taps - k
            acc = acc + jnp.dot(
                x_ref[start + shift : start + shift + ROW_TILE, :],
                wm_ref[k],
                preferred_element_type=jnp.float32,
            )
        o_ref[start : start + ROW_TILE, :] = acc


def masked_conv(window, responses, marks, rows):
    taps, coupled, ports = responses.shape
    weights = masked_weights_kernel(responses, marks)
    vmem = pl.BlockSpec(memory_space=pltpu.VMEM)
    return pl.pallas_call(
        conv_kernel,
        out_shape=jax.ShapeDtypeStruct((rows, ports), jnp.float32),
        in_specs=[vmem, vmem],
        out_specs=vmem,
        compiler_params=pltpu.CompilerParams(vmem_limit_bytes=48 * 1024 * 1024),
        cost_estimate=pl.CostEstimate(
            flops=2 * rows * taps * coupled * ports,
            transcendentals=0,
            bytes_accessed=window.size * 2 + responses.size * 2 + rows * ports * 4,
        ),
    )(window, weights)


def tap_marks(tap_counts, panel_links, first_tap, taps):
    tap_index = first_tap + jnp.arange(taps, dtype=jnp.int32)
    alive = tap_index[:, None] < tap_counts[None, :]
    lower = alive & (panel_links[None, :, 0] == 1)
    upper = alive & (panel_links[None, :, 1] == 1)
    marks = jnp.stack([lower, alive, upper], 1).astype(jnp.int32)
    return jnp.pad(marks, ((0, 0), (0, 5), (0, 0)))


def per_device(driven_wave, responses, tap_counts, panel_links):
    tap_dev = responses.shape[0]
    group_ports = driven_wave.shape[1]
    half_width = group_ports // 2
    n_tm = lax.axis_size("y") * lax.axis_size("zh") * lax.axis_size("core")
    total_taps = tap_dev * n_tm
    window_len = driven_wave.shape[0] * n_tm - total_taps
    me = tm_index()
    first_tap = me * tap_dev
    history = gather_history(extended(driven_wave, half_width))
    base = total_taps - first_tap - tap_dev
    window = lax.dynamic_slice_in_dim(history, base, window_len + tap_dev, 0)
    marks = tap_marks(tap_counts, panel_links, first_tap, tap_dev)
    partial = masked_conv(window, responses, marks, window_len)
    summed = reduce_scatter(partial, n_tm)
    return summed.astype(jnp.bfloat16)


def solution(mesh):
    band, tm = mesh.devices.shape
    view = Mesh(mesh.devices.reshape(band, tm // 8, 4, 2), ("band",) + TM)
    return jax.shard_map(
        per_device,
        mesh=view,
        in_specs=(P(TM, "band"), P(TM, None, "band"), P("band"), P("band", None)),
        out_specs=P(TM, "band"),
        check_vma=False,
    )
```

```python
import jax
import jax.numpy as jnp
from jax import lax
from jax.experimental import pallas as pl
from jax.experimental.pallas import tpu as pltpu
from jax.sharding import Mesh
from jax.sharding import PartitionSpec as P

TM = ("y", "zh", "core")


def extended(cells, width):
    count = lax.axis_size("band")
    ends = count - 1
    head = cells[:, :width]
    tail = cells[:, cells.shape[1] - width :]
    return jnp.concatenate(
        [
            lax.ppermute(tail, "band", [(i, (i + 1) % count) for i in range(ends)]),
            cells,
            lax.ppermute(head, "band", [((i + 1) % count, i) for i in range(ends)]),
        ],
        axis=1,
    )


def masked_weights(responses, tap_counts, panel_links, first_tap):
    tap_dev, coupled_ports, group_ports = responses.shape
    half_width = (coupled_ports - group_ports) // 2
    tap_index = first_tap + jnp.arange(tap_dev, dtype=jnp.int32)
    tap_alive = tap_index[:, None] < tap_counts[None, :]
    port_index = jnp.arange(coupled_ports, dtype=jnp.int32)[:, None]
    lower_open = panel_links[None, :, 0] == 1
    upper_open = panel_links[None, :, 1] == 1
    couple_open = jnp.where(
        port_index < half_width,
        lower_open,
        jnp.where(port_index >= half_width + group_ports, upper_open, True),
    )
    keep_mask = tap_alive[:, None, :] & couple_open[None, :, :]
    return jnp.where(keep_mask, responses, jnp.zeros_like(responses))


def swap_core(x):
    return lax.ppermute(x, "core", [(0, 1), (1, 0)])


def gather_history(x):
    chips = lax.axis_size("y") * lax.axis_size("zh")
    spread = jnp.broadcast_to(x[None], (chips,) + x.shape)
    mine = lax.all_to_all(spread, ("y", "zh"), 0, 0, tiled=True)
    other = swap_core(mine)
    first = lax.axis_index("core") == 0
    pair = jnp.stack([jnp.where(first, mine, other), jnp.where(first, other, mine)], 1)
    return pair.reshape(-1, x.shape[1])


def reduce_scatter(partial, n_tm):
    chips = n_tm // 2
    blocks = partial.reshape(chips, 2, partial.shape[0] // n_tm, partial.shape[1])
    first = lax.axis_index("core") == 0
    keep = jnp.where(first, blocks[:, 0], blocks[:, 1])
    give = jnp.where(first, blocks[:, 1], blocks[:, 0])
    combined = keep + swap_core(give)
    return lax.all_to_all(combined, ("y", "zh"), 0, 0, tiled=True).sum(0)


def tm_index():
    return (lax.axis_index("y") * lax.axis_size("zh") + lax.axis_index("zh")) * lax.axis_size(
        "core"
    ) + lax.axis_index("core")


ROW_TILE = 512


def conv_kernel(x_ref, w_ref, m_ref, o_ref, wm_ref):
    taps, coupled, ports = w_ref.shape
    half = (coupled - ports) // 2
    for k in range(taps):
        marks = m_ref[k]
        for lo, hi, row in ((0, half, 0), (half, half + ports, 1), (half + ports, coupled, 2)):
            keep = marks[row : row + 1, :] != 0
            block = w_ref[k, lo:hi, :]
            wm_ref[k, lo:hi, :] = jnp.where(keep, block, jnp.zeros_like(block))
    rows = o_ref.shape[0]
    for r in range(rows // ROW_TILE):
        start = r * ROW_TILE
        acc = jnp.zeros((ROW_TILE, ports), jnp.float32)
        for k in range(taps):
            shift = taps - k
            acc = acc + jnp.dot(
                x_ref[start + shift : start + shift + ROW_TILE, :],
                wm_ref[k],
                preferred_element_type=jnp.float32,
            )
        o_ref[start : start + ROW_TILE, :] = acc


def masked_conv(window, responses, marks, rows):
    taps, coupled, ports = responses.shape
    vmem = pl.BlockSpec(memory_space=pltpu.VMEM)
    return pl.pallas_call(
        conv_kernel,
        out_shape=jax.ShapeDtypeStruct((rows, ports), jnp.float32),
        in_specs=[vmem, vmem, vmem],
        out_specs=vmem,
        scratch_shapes=[pltpu.VMEM((taps, coupled, ports), responses.dtype)],
        compiler_params=pltpu.CompilerParams(vmem_limit_bytes=48 * 1024 * 1024),
        cost_estimate=pl.CostEstimate(
            flops=2 * rows * taps * coupled * ports,
            transcendentals=0,
            bytes_accessed=window.size * 2 + responses.size * 2 + rows * ports * 4,
        ),
    )(window, responses, marks)


def tap_marks(tap_counts, panel_links, first_tap, taps):
    tap_index = first_tap + jnp.arange(taps, dtype=jnp.int32)
    alive = tap_index[:, None] < tap_counts[None, :]
    lower = alive & (panel_links[None, :, 0] == 1)
    upper = alive & (panel_links[None, :, 1] == 1)
    marks = jnp.stack([lower, alive, upper], 1).astype(jnp.int32)
    return jnp.pad(marks, ((0, 0), (0, 5), (0, 0)))


def per_device(driven_wave, responses, tap_counts, panel_links):
    tap_dev = responses.shape[0]
    group_ports = driven_wave.shape[1]
    half_width = group_ports // 2
    n_tm = lax.axis_size("y") * lax.axis_size("zh") * lax.axis_size("core")
    total_taps = tap_dev * n_tm
    window_len = driven_wave.shape[0] * n_tm - total_taps
    me = tm_index()
    first_tap = me * tap_dev
    history = gather_history(extended(driven_wave, half_width))
    base = total_taps - first_tap - tap_dev
    window = lax.dynamic_slice_in_dim(history, base, window_len + tap_dev, 0)
    marks = tap_marks(tap_counts, panel_links, first_tap, tap_dev)
    partial = masked_conv(window, responses, marks, window_len)
    summed = reduce_scatter(partial, n_tm)
    return summed.astype(jnp.bfloat16)


def solution(mesh):
    band, tm = mesh.devices.shape
    view = Mesh(mesh.devices.reshape(band, tm // 8, 4, 2), ("band",) + TM)
    return jax.shard_map(
        per_device,
        mesh=view,
        in_specs=(P(TM, "band"), P(TM, None, "band"), P("band"), P("band", None)),
        out_specs=P(TM, "band"),
        check_vma=False,
    )
```

```python
import jax
import jax.numpy as jnp
from jax import lax
from jax.experimental import pallas as pl
from jax.experimental.pallas import tpu as pltpu
from jax.sharding import Mesh
from jax.sharding import PartitionSpec as P

TM = ("y", "zh", "core")


def extended(cells, width):
    count = lax.axis_size("band")
    ends = count - 1
    head = cells[:, :width]
    tail = cells[:, cells.shape[1] - width :]
    return jnp.concatenate(
        [
            lax.ppermute(tail, "band", [(i, (i + 1) % count) for i in range(ends)]),
            cells,
            lax.ppermute(head, "band", [((i + 1) % count, i) for i in range(ends)]),
        ],
        axis=1,
    )


def masked_weights(responses, tap_counts, panel_links, first_tap):
    tap_dev, coupled_ports, group_ports = responses.shape
    half_width = (coupled_ports - group_ports) // 2
    tap_index = first_tap + jnp.arange(tap_dev, dtype=jnp.int32)
    tap_alive = tap_index[:, None] < tap_counts[None, :]
    port_index = jnp.arange(coupled_ports, dtype=jnp.int32)[:, None]
    lower_open = panel_links[None, :, 0] == 1
    upper_open = panel_links[None, :, 1] == 1
    couple_open = jnp.where(
        port_index < half_width,
        lower_open,
        jnp.where(port_index >= half_width + group_ports, upper_open, True),
    )
    keep_mask = tap_alive[:, None, :] & couple_open[None, :, :]
    return jnp.where(keep_mask, responses, jnp.zeros_like(responses))


def swap_core(x):
    return lax.ppermute(x, "core", [(0, 1), (1, 0)])


def gather_window(x, base, length, align):
    chips = lax.axis_size("y") * lax.axis_size("zh")
    spread = jnp.broadcast_to(x[None], (chips,) + x.shape)
    mine = lax.all_to_all(spread, ("y", "zh"), 0, 0, tiled=True)
    pair_rows = 2 * x.shape[0]
    span = (length + 2 * pair_rows - align - 1) // pair_rows
    first_pair = jnp.minimum(base // pair_rows, chips - span)
    needed = lax.dynamic_slice_in_dim(mine, first_pair, span, 0)
    other = swap_core(needed)
    first = lax.axis_index("core") == 0
    pair = jnp.stack([jnp.where(first, needed, other), jnp.where(first, other, needed)], 1)
    rows = pair.reshape(-1, x.shape[1])
    return lax.dynamic_slice_in_dim(rows, base - first_pair * pair_rows, length, 0)


def reduce_scatter(partial, n_tm):
    chips = n_tm // 2
    blocks = partial.reshape(chips, 2, partial.shape[0] // n_tm, partial.shape[1])
    first = lax.axis_index("core") == 0
    keep = jnp.where(first, blocks[:, 0], blocks[:, 1])
    give = jnp.where(first, blocks[:, 1], blocks[:, 0])
    combined = keep + swap_core(give)
    return lax.all_to_all(combined, ("y", "zh"), 0, 0, tiled=True).sum(0)


def tm_index():
    return (lax.axis_index("y") * lax.axis_size("zh") + lax.axis_index("zh")) * lax.axis_size(
        "core"
    ) + lax.axis_index("core")


ROW_TILE = 512


def conv_kernel(x_ref, w_ref, m_ref, o_ref, wm_ref):
    taps, coupled, ports = w_ref.shape
    half = (coupled - ports) // 2
    for k in range(taps):
        marks = m_ref[k]
        for lo, hi, row in ((0, half, 0), (half, half + ports, 1), (half + ports, coupled, 2)):
            keep = marks[row : row + 1, :] != 0
            block = w_ref[k, lo:hi, :]
            wm_ref[k, lo:hi, :] = jnp.where(keep, block, jnp.zeros_like(block))
    rows = o_ref.shape[0]
    for r in range(rows // ROW_TILE):
        start = r * ROW_TILE
        acc = jnp.zeros((ROW_TILE, ports), jnp.float32)
        for k in range(taps):
            shift = taps - k
            acc = acc + jnp.dot(
                x_ref[start + shift : start + shift + ROW_TILE, :],
                wm_ref[k],
                preferred_element_type=jnp.float32,
            )
        o_ref[start : start + ROW_TILE, :] = acc


def masked_conv(window, responses, marks, rows):
    taps, coupled, ports = responses.shape
    vmem = pl.BlockSpec(memory_space=pltpu.VMEM)
    return pl.pallas_call(
        conv_kernel,
        out_shape=jax.ShapeDtypeStruct((rows, ports), jnp.float32),
        in_specs=[vmem, vmem, vmem],
        out_specs=vmem,
        scratch_shapes=[pltpu.VMEM((taps, coupled, ports), responses.dtype)],
        compiler_params=pltpu.CompilerParams(vmem_limit_bytes=48 * 1024 * 1024),
        cost_estimate=pl.CostEstimate(
            flops=2 * rows * taps * coupled * ports,
            transcendentals=0,
            bytes_accessed=window.size * 2 + responses.size * 2 + rows * ports * 4,
        ),
    )(window, responses, marks)


def tap_marks(tap_counts, panel_links, first_tap, taps):
    tap_index = first_tap + jnp.arange(taps, dtype=jnp.int32)
    alive = tap_index[:, None] < tap_counts[None, :]
    lower = alive & (panel_links[None, :, 0] == 1)
    upper = alive & (panel_links[None, :, 1] == 1)
    marks = jnp.stack([lower, alive, upper], 1).astype(jnp.int32)
    return jnp.pad(marks, ((0, 0), (0, 5), (0, 0)))


def per_device(driven_wave, responses, tap_counts, panel_links):
    tap_dev = responses.shape[0]
    group_ports = driven_wave.shape[1]
    half_width = group_ports // 2
    n_tm = lax.axis_size("y") * lax.axis_size("zh") * lax.axis_size("core")
    total_taps = tap_dev * n_tm
    window_len = driven_wave.shape[0] * n_tm - total_taps
    me = tm_index()
    first_tap = me * tap_dev
    base = total_taps - first_tap - tap_dev
    window = gather_window(extended(driven_wave, half_width), base, window_len + tap_dev, tap_dev)
    marks = tap_marks(tap_counts, panel_links, first_tap, tap_dev)
    partial = masked_conv(window, responses, marks, window_len)
    summed = reduce_scatter(partial, n_tm)
    return summed.astype(jnp.bfloat16)


def solution(mesh):
    band, tm = mesh.devices.shape
    view = Mesh(mesh.devices.reshape(band, tm // 8, 4, 2), ("band",) + TM)
    return jax.shard_map(
        per_device,
        mesh=view,
        in_specs=(P(TM, "band"), P(TM, None, "band"), P("band"), P("band", None)),
        out_specs=P(TM, "band"),
        check_vma=False,
    )
```

```python
import jax
import jax.numpy as jnp
from jax import lax
from jax.experimental import pallas as pl
from jax.experimental.pallas import tpu as pltpu
from jax.sharding import Mesh
from jax.sharding import PartitionSpec as P

TM = ("y", "zh", "core")


def extended(cells, width):
    count = lax.axis_size("band")
    ends = count - 1
    head = cells[:, :width]
    tail = cells[:, cells.shape[1] - width :]
    return jnp.concatenate(
        [
            lax.ppermute(tail, "band", [(i, (i + 1) % count) for i in range(ends)]),
            cells,
            lax.ppermute(head, "band", [((i + 1) % count, i) for i in range(ends)]),
        ],
        axis=1,
    )


def masked_weights(responses, tap_counts, panel_links, first_tap):
    tap_dev, coupled_ports, group_ports = responses.shape
    half_width = (coupled_ports - group_ports) // 2
    tap_index = first_tap + jnp.arange(tap_dev, dtype=jnp.int32)
    tap_alive = tap_index[:, None] < tap_counts[None, :]
    port_index = jnp.arange(coupled_ports, dtype=jnp.int32)[:, None]
    lower_open = panel_links[None, :, 0] == 1
    upper_open = panel_links[None, :, 1] == 1
    couple_open = jnp.where(
        port_index < half_width,
        lower_open,
        jnp.where(port_index >= half_width + group_ports, upper_open, True),
    )
    keep_mask = tap_alive[:, None, :] & couple_open[None, :, :]
    return jnp.where(keep_mask, responses, jnp.zeros_like(responses))


def swap_core(x):
    return lax.ppermute(x, "core", [(0, 1), (1, 0)])


def band_halo(cells, width):
    count = lax.axis_size("band")
    ends = count - 1
    head = cells[..., :width]
    tail = cells[..., cells.shape[-1] - width :]
    below = lax.ppermute(tail, "band", [(i, (i + 1) % count) for i in range(ends)])
    above = lax.ppermute(head, "band", [((i + 1) % count, i) for i in range(ends)])
    return jnp.concatenate([below, cells, above], axis=-1)


def gather_window(x, base, length, align, width):
    chips = lax.axis_size("y") * lax.axis_size("zh")
    spread = jnp.broadcast_to(x[None], (chips,) + x.shape)
    mine = lax.all_to_all(spread, ("y", "zh"), 0, 0, tiled=True)
    pair_rows = 2 * x.shape[0]
    span = (length + 2 * pair_rows - align - 1) // pair_rows
    first_pair = jnp.minimum(base // pair_rows, chips - span)
    needed = band_halo(lax.dynamic_slice_in_dim(mine, first_pair, span, 0), width)
    other = swap_core(needed)
    first = lax.axis_index("core") == 0
    pair = jnp.stack([jnp.where(first, needed, other), jnp.where(first, other, needed)], 1)
    rows = pair.reshape(-1, needed.shape[-1])
    return lax.dynamic_slice_in_dim(rows, base - first_pair * pair_rows, length, 0)


def reduce_scatter(partial, n_tm):
    chips = n_tm // 2
    blocks = partial.reshape(chips, 2, partial.shape[0] // n_tm, partial.shape[1])
    first = lax.axis_index("core") == 0
    keep = jnp.where(first, blocks[:, 0], blocks[:, 1])
    give = jnp.where(first, blocks[:, 1], blocks[:, 0])
    combined = keep + swap_core(give)
    return lax.all_to_all(combined, ("y", "zh"), 0, 0, tiled=True).sum(0)


def tm_index():
    return (lax.axis_index("y") * lax.axis_size("zh") + lax.axis_index("zh")) * lax.axis_size(
        "core"
    ) + lax.axis_index("core")


ROW_TILE = 512


def conv_kernel(x_ref, w_ref, m_ref, o_ref, wm_ref):
    taps, coupled, ports = w_ref.shape
    half = (coupled - ports) // 2
    for k in range(taps):
        marks = m_ref[k]
        for lo, hi, row in ((0, half, 0), (half, half + ports, 1), (half + ports, coupled, 2)):
            keep = marks[row : row + 1, :] != 0
            block = w_ref[k, lo:hi, :]
            wm_ref[k, lo:hi, :] = jnp.where(keep, block, jnp.zeros_like(block))
    rows = o_ref.shape[0]
    for r in range(rows // ROW_TILE):
        start = r * ROW_TILE
        acc = jnp.zeros((ROW_TILE, ports), jnp.float32)
        for k in range(taps):
            shift = taps - k
            acc = acc + jnp.dot(
                x_ref[start + shift : start + shift + ROW_TILE, :],
                wm_ref[k],
                preferred_element_type=jnp.float32,
            )
        o_ref[start : start + ROW_TILE, :] = acc


def masked_conv(window, responses, marks, rows):
    taps, coupled, ports = responses.shape
    vmem = pl.BlockSpec(memory_space=pltpu.VMEM)
    return pl.pallas_call(
        conv_kernel,
        out_shape=jax.ShapeDtypeStruct((rows, ports), jnp.float32),
        in_specs=[vmem, vmem, vmem],
        out_specs=vmem,
        scratch_shapes=[pltpu.VMEM((taps, coupled, ports), responses.dtype)],
        compiler_params=pltpu.CompilerParams(vmem_limit_bytes=48 * 1024 * 1024),
        cost_estimate=pl.CostEstimate(
            flops=2 * rows * taps * coupled * ports,
            transcendentals=0,
            bytes_accessed=window.size * 2 + responses.size * 2 + rows * ports * 4,
        ),
    )(window, responses, marks)


def tap_marks(tap_counts, panel_links, first_tap, taps):
    tap_index = first_tap + jnp.arange(taps, dtype=jnp.int32)
    alive = tap_index[:, None] < tap_counts[None, :]
    lower = alive & (panel_links[None, :, 0] == 1)
    upper = alive & (panel_links[None, :, 1] == 1)
    marks = jnp.stack([lower, alive, upper], 1).astype(jnp.int32)
    return jnp.pad(marks, ((0, 0), (0, 5), (0, 0)))


def per_device(driven_wave, responses, tap_counts, panel_links):
    tap_dev = responses.shape[0]
    group_ports = driven_wave.shape[1]
    half_width = group_ports // 2
    n_tm = lax.axis_size("y") * lax.axis_size("zh") * lax.axis_size("core")
    total_taps = tap_dev * n_tm
    window_len = driven_wave.shape[0] * n_tm - total_taps
    me = tm_index()
    first_tap = me * tap_dev
    base = total_taps - first_tap - tap_dev
    window = gather_window(driven_wave, base, window_len + tap_dev, tap_dev, half_width)
    marks = tap_marks(tap_counts, panel_links, first_tap, tap_dev)
    partial = masked_conv(window, responses, marks, window_len)
    summed = reduce_scatter(partial, n_tm)
    return summed.astype(jnp.bfloat16)


def solution(mesh):
    band, tm = mesh.devices.shape
    view = Mesh(mesh.devices.reshape(band, tm // 8, 4, 2), ("band",) + TM)
    return jax.shard_map(
        per_device,
        mesh=view,
        in_specs=(P(TM, "band"), P(TM, None, "band"), P("band"), P("band", None)),
        out_specs=P(TM, "band"),
        check_vma=False,
    )
```

```python
import jax
import jax.numpy as jnp
from jax import lax
from jax.experimental import pallas as pl
from jax.experimental.pallas import tpu as pltpu
from jax.sharding import Mesh
from jax.sharding import PartitionSpec as P

TM = ("y", "zh", "core")


def extended(cells, width):
    count = lax.axis_size("band")
    ends = count - 1
    head = cells[:, :width]
    tail = cells[:, cells.shape[1] - width :]
    return jnp.concatenate(
        [
            lax.ppermute(tail, "band", [(i, (i + 1) % count) for i in range(ends)]),
            cells,
            lax.ppermute(head, "band", [((i + 1) % count, i) for i in range(ends)]),
        ],
        axis=1,
    )


def masked_weights(responses, tap_counts, panel_links, first_tap):
    tap_dev, coupled_ports, group_ports = responses.shape
    half_width = (coupled_ports - group_ports) // 2
    tap_index = first_tap + jnp.arange(tap_dev, dtype=jnp.int32)
    tap_alive = tap_index[:, None] < tap_counts[None, :]
    port_index = jnp.arange(coupled_ports, dtype=jnp.int32)[:, None]
    lower_open = panel_links[None, :, 0] == 1
    upper_open = panel_links[None, :, 1] == 1
    couple_open = jnp.where(
        port_index < half_width,
        lower_open,
        jnp.where(port_index >= half_width + group_ports, upper_open, True),
    )
    keep_mask = tap_alive[:, None, :] & couple_open[None, :, :]
    return jnp.where(keep_mask, responses, jnp.zeros_like(responses))


def swap_core(x):
    return lax.ppermute(x, "core", [(0, 1), (1, 0)])


def band_halo(cells, width, flip):
    count = lax.axis_size("band")
    cores = lax.axis_size("core")
    head = cells[..., :width]
    tail = cells[..., cells.shape[-1] - width :]
    up = [
        (b * cores + k, (b + 1) * cores + (k + flip) % cores)
        for b in range(count - 1)
        for k in range(cores)
    ]
    down = [(dst, src) for src, dst in up]
    below = lax.ppermute(tail, ("band", "core"), up)
    above = lax.ppermute(head, ("band", "core"), down)
    return below, above


def gather_window(x, base, length, align, width):
    chips = lax.axis_size("y") * lax.axis_size("zh")
    spread = jnp.broadcast_to(x[None], (chips,) + x.shape)
    mine = lax.all_to_all(spread, ("y", "zh"), 0, 0, tiled=True)
    pair_rows = 2 * x.shape[0]
    span = (length + 2 * pair_rows - align - 1) // pair_rows
    first_pair = jnp.minimum(base // pair_rows, chips - span)
    needed = lax.dynamic_slice_in_dim(mine, first_pair, span, 0)
    other = swap_core(needed)
    below, above = band_halo(needed, width, 0)
    below_other, above_other = band_halo(needed, width, 1)
    needed = jnp.concatenate([below, needed, above], axis=-1)
    other = jnp.concatenate([below_other, other, above_other], axis=-1)
    first = lax.axis_index("core") == 0
    pair = jnp.stack([jnp.where(first, needed, other), jnp.where(first, other, needed)], 1)
    rows = pair.reshape(-1, needed.shape[-1])
    return lax.dynamic_slice_in_dim(rows, base - first_pair * pair_rows, length, 0)


def reduce_scatter(partial, n_tm):
    chips = n_tm // 2
    blocks = partial.reshape(chips, 2, partial.shape[0] // n_tm, partial.shape[1])
    first = lax.axis_index("core") == 0
    keep = jnp.where(first, blocks[:, 0], blocks[:, 1])
    give = jnp.where(first, blocks[:, 1], blocks[:, 0])
    combined = keep + swap_core(give)
    return lax.all_to_all(combined, ("y", "zh"), 0, 0, tiled=True).sum(0)


def tm_index():
    return (lax.axis_index("y") * lax.axis_size("zh") + lax.axis_index("zh")) * lax.axis_size(
        "core"
    ) + lax.axis_index("core")


ROW_TILE = 512


def conv_kernel(x_ref, w_ref, m_ref, o_ref, wm_ref):
    taps, coupled, ports = w_ref.shape
    half = (coupled - ports) // 2
    for k in range(taps):
        marks = m_ref[k]
        for lo, hi, row in ((0, half, 0), (half, half + ports, 1), (half + ports, coupled, 2)):
            keep = marks[row : row + 1, :] != 0
            block = w_ref[k, lo:hi, :]
            wm_ref[k, lo:hi, :] = jnp.where(keep, block, jnp.zeros_like(block))
    rows = o_ref.shape[0]
    for r in range(rows // ROW_TILE):
        start = r * ROW_TILE
        acc = jnp.zeros((ROW_TILE, ports), jnp.float32)
        for k in range(taps):
            shift = taps - k
            acc = acc + jnp.dot(
                x_ref[start + shift : start + shift + ROW_TILE, :],
                wm_ref[k],
                preferred_element_type=jnp.float32,
            )
        o_ref[start : start + ROW_TILE, :] = acc


def masked_conv(window, responses, marks, rows):
    taps, coupled, ports = responses.shape
    vmem = pl.BlockSpec(memory_space=pltpu.VMEM)
    return pl.pallas_call(
        conv_kernel,
        out_shape=jax.ShapeDtypeStruct((rows, ports), jnp.float32),
        in_specs=[vmem, vmem, vmem],
        out_specs=vmem,
        scratch_shapes=[pltpu.VMEM((taps, coupled, ports), responses.dtype)],
        compiler_params=pltpu.CompilerParams(vmem_limit_bytes=48 * 1024 * 1024),
        cost_estimate=pl.CostEstimate(
            flops=2 * rows * taps * coupled * ports,
            transcendentals=0,
            bytes_accessed=window.size * 2 + responses.size * 2 + rows * ports * 4,
        ),
    )(window, responses, marks)


def tap_marks(tap_counts, panel_links, first_tap, taps):
    tap_index = first_tap + jnp.arange(taps, dtype=jnp.int32)
    alive = tap_index[:, None] < tap_counts[None, :]
    lower = alive & (panel_links[None, :, 0] == 1)
    upper = alive & (panel_links[None, :, 1] == 1)
    marks = jnp.stack([lower, alive, upper], 1).astype(jnp.int32)
    return jnp.pad(marks, ((0, 0), (0, 5), (0, 0)))


def per_device(driven_wave, responses, tap_counts, panel_links):
    tap_dev = responses.shape[0]
    group_ports = driven_wave.shape[1]
    half_width = group_ports // 2
    n_tm = lax.axis_size("y") * lax.axis_size("zh") * lax.axis_size("core")
    total_taps = tap_dev * n_tm
    window_len = driven_wave.shape[0] * n_tm - total_taps
    me = tm_index()
    first_tap = me * tap_dev
    base = total_taps - first_tap - tap_dev
    window = gather_window(driven_wave, base, window_len + tap_dev, tap_dev, half_width)
    marks = tap_marks(tap_counts, panel_links, first_tap, tap_dev)
    partial = masked_conv(window, responses, marks, window_len)
    summed = reduce_scatter(partial, n_tm)
    return summed.astype(jnp.bfloat16)


def solution(mesh):
    band, tm = mesh.devices.shape
    view = Mesh(mesh.devices.reshape(band, tm // 8, 4, 2), ("band",) + TM)
    return jax.shard_map(
        per_device,
        mesh=view,
        in_specs=(P(TM, "band"), P(TM, None, "band"), P("band"), P("band", None)),
        out_specs=P(TM, "band"),
        check_vma=False,
    )
```

```python
import jax
import jax.numpy as jnp
from jax import lax
from jax.experimental import pallas as pl
from jax.experimental.pallas import tpu as pltpu
from jax.sharding import Mesh
from jax.sharding import PartitionSpec as P

TM = ("y", "zh", "core")


def extended(cells, width):
    count = lax.axis_size("band")
    ends = count - 1
    head = cells[:, :width]
    tail = cells[:, cells.shape[1] - width :]
    return jnp.concatenate(
        [
            lax.ppermute(tail, "band", [(i, (i + 1) % count) for i in range(ends)]),
            cells,
            lax.ppermute(head, "band", [((i + 1) % count, i) for i in range(ends)]),
        ],
        axis=1,
    )


def masked_weights(responses, tap_counts, panel_links, first_tap):
    tap_dev, coupled_ports, group_ports = responses.shape
    half_width = (coupled_ports - group_ports) // 2
    tap_index = first_tap + jnp.arange(tap_dev, dtype=jnp.int32)
    tap_alive = tap_index[:, None] < tap_counts[None, :]
    port_index = jnp.arange(coupled_ports, dtype=jnp.int32)[:, None]
    lower_open = panel_links[None, :, 0] == 1
    upper_open = panel_links[None, :, 1] == 1
    couple_open = jnp.where(
        port_index < half_width,
        lower_open,
        jnp.where(port_index >= half_width + group_ports, upper_open, True),
    )
    keep_mask = tap_alive[:, None, :] & couple_open[None, :, :]
    return jnp.where(keep_mask, responses, jnp.zeros_like(responses))


def swap_core(x):
    return lax.ppermute(x, "core", [(0, 1), (1, 0)])


def band_halo(cells, width):
    count = lax.axis_size("band")
    ends = count - 1
    head = cells[..., :width]
    tail = cells[..., cells.shape[-1] - width :]
    below = lax.ppermute(tail, "band", [(i, (i + 1) % count) for i in range(ends)])
    above = lax.ppermute(head, "band", [((i + 1) % count, i) for i in range(ends)])
    return jnp.concatenate([below, cells, above], axis=-1)


def copies_kernel(x_ref, o_ref):
    for c in range(o_ref.shape[0]):
        o_ref[c] = x_ref[...]


def copies(x, count):
    vmem = pl.BlockSpec(memory_space=pltpu.VMEM)
    return pl.pallas_call(
        copies_kernel,
        out_shape=jax.ShapeDtypeStruct((count,) + x.shape, x.dtype),
        in_specs=[vmem],
        out_specs=vmem,
        cost_estimate=pl.CostEstimate(
            flops=0, transcendentals=0, bytes_accessed=(count + 1) * x.size * 2
        ),
    )(x)


def gather_window(x, base, length, align, width):
    chips = lax.axis_size("y") * lax.axis_size("zh")
    spread = copies(x, chips)
    mine = lax.all_to_all(spread, ("y", "zh"), 0, 0, tiled=True)
    pair_rows = 2 * x.shape[0]
    span = (length + 2 * pair_rows - align - 1) // pair_rows
    first_pair = jnp.minimum(base // pair_rows, chips - span)
    needed = band_halo(lax.dynamic_slice_in_dim(mine, first_pair, span, 0), width)
    other = swap_core(needed)
    first = lax.axis_index("core") == 0
    pair = jnp.stack([jnp.where(first, needed, other), jnp.where(first, other, needed)], 1)
    rows = pair.reshape(-1, needed.shape[-1])
    return lax.dynamic_slice_in_dim(rows, base - first_pair * pair_rows, length, 0)


def reduce_scatter(partial, n_tm):
    chips = n_tm // 2
    blocks = partial.reshape(chips, 2, partial.shape[0] // n_tm, partial.shape[1])
    first = lax.axis_index("core") == 0
    keep = jnp.where(first, blocks[:, 0], blocks[:, 1])
    give = jnp.where(first, blocks[:, 1], blocks[:, 0])
    combined = keep + swap_core(give)
    return lax.all_to_all(combined, ("y", "zh"), 0, 0, tiled=True).sum(0)


def tm_index():
    return (lax.axis_index("y") * lax.axis_size("zh") + lax.axis_index("zh")) * lax.axis_size(
        "core"
    ) + lax.axis_index("core")


ROW_TILE = 512


def conv_kernel(x_ref, w_ref, m_ref, o_ref, wm_ref):
    taps, coupled, ports = w_ref.shape
    half = (coupled - ports) // 2
    for k in range(taps):
        marks = m_ref[k]
        for lo, hi, row in ((0, half, 0), (half, half + ports, 1), (half + ports, coupled, 2)):
            keep = marks[row : row + 1, :] != 0
            block = w_ref[k, lo:hi, :]
            wm_ref[k, lo:hi, :] = jnp.where(keep, block, jnp.zeros_like(block))
    rows = o_ref.shape[0]
    for r in range(rows // ROW_TILE):
        start = r * ROW_TILE
        acc = jnp.zeros((ROW_TILE, ports), jnp.float32)
        for k in range(taps):
            shift = taps - k
            acc = acc + jnp.dot(
                x_ref[start + shift : start + shift + ROW_TILE, :],
                wm_ref[k],
                preferred_element_type=jnp.float32,
            )
        o_ref[start : start + ROW_TILE, :] = acc


def masked_conv(window, responses, marks, rows):
    taps, coupled, ports = responses.shape
    vmem = pl.BlockSpec(memory_space=pltpu.VMEM)
    return pl.pallas_call(
        conv_kernel,
        out_shape=jax.ShapeDtypeStruct((rows, ports), jnp.float32),
        in_specs=[vmem, vmem, vmem],
        out_specs=vmem,
        scratch_shapes=[pltpu.VMEM((taps, coupled, ports), responses.dtype)],
        compiler_params=pltpu.CompilerParams(vmem_limit_bytes=48 * 1024 * 1024),
        cost_estimate=pl.CostEstimate(
            flops=2 * rows * taps * coupled * ports,
            transcendentals=0,
            bytes_accessed=window.size * 2 + responses.size * 2 + rows * ports * 4,
        ),
    )(window, responses, marks)


def tap_marks(tap_counts, panel_links, first_tap, taps):
    tap_index = first_tap + jnp.arange(taps, dtype=jnp.int32)
    alive = tap_index[:, None] < tap_counts[None, :]
    lower = alive & (panel_links[None, :, 0] == 1)
    upper = alive & (panel_links[None, :, 1] == 1)
    marks = jnp.stack([lower, alive, upper], 1).astype(jnp.int32)
    return jnp.pad(marks, ((0, 0), (0, 5), (0, 0)))


def per_device(driven_wave, responses, tap_counts, panel_links):
    tap_dev = responses.shape[0]
    group_ports = driven_wave.shape[1]
    half_width = group_ports // 2
    n_tm = lax.axis_size("y") * lax.axis_size("zh") * lax.axis_size("core")
    total_taps = tap_dev * n_tm
    window_len = driven_wave.shape[0] * n_tm - total_taps
    me = tm_index()
    first_tap = me * tap_dev
    base = total_taps - first_tap - tap_dev
    window = gather_window(driven_wave, base, window_len + tap_dev, tap_dev, half_width)
    marks = tap_marks(tap_counts, panel_links, first_tap, tap_dev)
    partial = masked_conv(window, responses, marks, window_len)
    summed = reduce_scatter(partial, n_tm)
    return summed.astype(jnp.bfloat16)


def solution(mesh):
    band, tm = mesh.devices.shape
    view = Mesh(mesh.devices.reshape(band, tm // 8, 4, 2), ("band",) + TM)
    return jax.shard_map(
        per_device,
        mesh=view,
        in_specs=(P(TM, "band"), P(TM, None, "band"), P("band"), P("band", None)),
        out_specs=P(TM, "band"),
        check_vma=False,
    )
```

```python
import functools

import jax
import jax.numpy as jnp
from jax import lax
from jax.experimental import pallas as pl
from jax.experimental.pallas import tpu as pltpu
from jax.sharding import Mesh
from jax.sharding import PartitionSpec as P

TM = ("y", "zh", "core")


def extended(cells, width):
    count = lax.axis_size("band")
    ends = count - 1
    head = cells[:, :width]
    tail = cells[:, cells.shape[1] - width :]
    return jnp.concatenate(
        [
            lax.ppermute(tail, "band", [(i, (i + 1) % count) for i in range(ends)]),
            cells,
            lax.ppermute(head, "band", [((i + 1) % count, i) for i in range(ends)]),
        ],
        axis=1,
    )


def masked_weights(responses, tap_counts, panel_links, first_tap):
    tap_dev, coupled_ports, group_ports = responses.shape
    half_width = (coupled_ports - group_ports) // 2
    tap_index = first_tap + jnp.arange(tap_dev, dtype=jnp.int32)
    tap_alive = tap_index[:, None] < tap_counts[None, :]
    port_index = jnp.arange(coupled_ports, dtype=jnp.int32)[:, None]
    lower_open = panel_links[None, :, 0] == 1
    upper_open = panel_links[None, :, 1] == 1
    couple_open = jnp.where(
        port_index < half_width,
        lower_open,
        jnp.where(port_index >= half_width + group_ports, upper_open, True),
    )
    keep_mask = tap_alive[:, None, :] & couple_open[None, :, :]
    return jnp.where(keep_mask, responses, jnp.zeros_like(responses))


def swap_core(x):
    return lax.ppermute(x, "core", [(0, 1), (1, 0)])


def band_halo(cells, width):
    count = lax.axis_size("band")
    ends = count - 1
    head = cells[..., :width]
    tail = cells[..., cells.shape[-1] - width :]
    below = lax.ppermute(tail, "band", [(i, (i + 1) % count) for i in range(ends)])
    above = lax.ppermute(head, "band", [((i + 1) % count, i) for i in range(ends)])
    return jnp.concatenate([below, above], axis=-1)


def assemble(needed, base, first_pair, pair_rows, length):
    other = swap_core(needed)
    first = lax.axis_index("core") == 0
    pair = jnp.stack([jnp.where(first, needed, other), jnp.where(first, other, needed)], 1)
    rows = pair.reshape(-1, needed.shape[-1])
    return lax.dynamic_slice_in_dim(rows, base - first_pair * pair_rows, length, 0)


def split_windows(x, base, length, align, width):
    chips = lax.axis_size("y") * lax.axis_size("zh")
    spread = jnp.broadcast_to(x[None], (chips,) + x.shape)
    mine = lax.all_to_all(spread, ("y", "zh"), 0, 0, tiled=True)
    pair_rows = 2 * x.shape[0]
    span = (length + 2 * pair_rows - align - 1) // pair_rows
    first_pair = jnp.minimum(base // pair_rows, chips - span)
    needed = lax.dynamic_slice_in_dim(mine, first_pair, span, 0)
    edges = band_halo(needed, width)
    own = assemble(needed, base, first_pair, pair_rows, length)
    return own, lambda edges: assemble(edges, base, first_pair, pair_rows, length), edges


def reduce_scatter(partial, n_tm):
    chips = n_tm // 2
    blocks = partial.reshape(chips, 2, partial.shape[0] // n_tm, partial.shape[1])
    first = lax.axis_index("core") == 0
    keep = jnp.where(first, blocks[:, 0], blocks[:, 1])
    give = jnp.where(first, blocks[:, 1], blocks[:, 0])
    combined = keep + swap_core(give)
    return lax.all_to_all(combined, ("y", "zh"), 0, 0, tiled=True).sum(0)


def tm_index():
    return (lax.axis_index("y") * lax.axis_size("zh") + lax.axis_index("zh")) * lax.axis_size(
        "core"
    ) + lax.axis_index("core")


ROW_TILE = 512


def conv_kernel(segments, x_ref, w_ref, m_ref, *refs):
    if len(refs) == 3:
        acc_ref, o_ref, wm_ref = refs
    else:
        acc_ref = None
        o_ref, wm_ref = refs
    taps = w_ref.shape[0]
    ports = o_ref.shape[1]
    for k in range(taps):
        marks = m_ref[k]
        for lo, hi, row, at in segments:
            keep = marks[row : row + 1, :] != 0
            block = w_ref[k, lo:hi, :]
            wm_ref[k, at : at + hi - lo, :] = jnp.where(keep, block, jnp.zeros_like(block))
    rows = o_ref.shape[0]
    for r in range(rows // ROW_TILE):
        start = r * ROW_TILE
        if acc_ref is None:
            acc = jnp.zeros((ROW_TILE, ports), jnp.float32)
        else:
            acc = acc_ref[start : start + ROW_TILE, :]
        for k in range(taps):
            shift = taps - k
            acc = acc + jnp.dot(
                x_ref[start + shift : start + shift + ROW_TILE, :],
                wm_ref[k],
                preferred_element_type=jnp.float32,
            )
        o_ref[start : start + ROW_TILE, :] = acc


def conv_part(window, responses, marks, rows, segments, acc=None):
    taps, coupled, ports = responses.shape
    depth = window.shape[1]
    vmem = pl.BlockSpec(memory_space=pltpu.VMEM)
    operands = [window, responses, marks] + ([] if acc is None else [acc])
    return pl.pallas_call(
        functools.partial(conv_kernel, segments),
        out_shape=jax.ShapeDtypeStruct((rows, ports), jnp.float32),
        in_specs=[vmem] * len(operands),
        out_specs=vmem,
        scratch_shapes=[pltpu.VMEM((taps, depth, ports), responses.dtype)],
        input_output_aliases={} if acc is None else {3: 0},
        compiler_params=pltpu.CompilerParams(vmem_limit_bytes=48 * 1024 * 1024),
        cost_estimate=pl.CostEstimate(
            flops=2 * rows * taps * depth * ports,
            transcendentals=0,
            bytes_accessed=window.size * 2 + taps * depth * ports * 2 + rows * ports * 4,
        ),
    )(*operands)


def tap_marks(tap_counts, panel_links, first_tap, taps):
    tap_index = first_tap + jnp.arange(taps, dtype=jnp.int32)
    alive = tap_index[:, None] < tap_counts[None, :]
    lower = alive & (panel_links[None, :, 0] == 1)
    upper = alive & (panel_links[None, :, 1] == 1)
    marks = jnp.stack([lower, alive, upper], 1).astype(jnp.int32)
    return jnp.pad(marks, ((0, 0), (0, 5), (0, 0)))


def per_device(driven_wave, responses, tap_counts, panel_links):
    tap_dev = responses.shape[0]
    group_ports = driven_wave.shape[1]
    half_width = group_ports // 2
    n_tm = lax.axis_size("y") * lax.axis_size("zh") * lax.axis_size("core")
    total_taps = tap_dev * n_tm
    window_len = driven_wave.shape[0] * n_tm - total_taps
    me = tm_index()
    first_tap = me * tap_dev
    base = total_taps - first_tap - tap_dev
    own, halo_of, edges = split_windows(driven_wave, base, window_len + tap_dev, tap_dev, half_width)
    marks = tap_marks(tap_counts, panel_links, first_tap, tap_dev)
    ports = group_ports
    partial = conv_part(own, responses, marks, window_len, ((half_width, half_width + ports, 1, 0),))
    partial, edges = lax.optimization_barrier((partial, edges))
    partial = conv_part(
        halo_of(edges),
        responses,
        marks,
        window_len,
        ((0, half_width, 0, 0), (half_width + ports, 2 * ports, 2, half_width)),
        partial,
    )
    summed = reduce_scatter(partial, n_tm)
    return summed.astype(jnp.bfloat16)


def solution(mesh):
    band, tm = mesh.devices.shape
    view = Mesh(mesh.devices.reshape(band, tm // 8, 4, 2), ("band",) + TM)
    return jax.shard_map(
        per_device,
        mesh=view,
        in_specs=(P(TM, "band"), P(TM, None, "band"), P("band"), P("band", None)),
        out_specs=P(TM, "band"),
        check_vma=False,
    )
```

```python
import functools

import jax
import jax.numpy as jnp
from jax import lax
from jax.experimental import pallas as pl
from jax.experimental.pallas import tpu as pltpu
from jax.sharding import Mesh
from jax.sharding import PartitionSpec as P

TM = ("y", "zh", "core")


def extended(cells, width):
    count = lax.axis_size("band")
    ends = count - 1
    head = cells[:, :width]
    tail = cells[:, cells.shape[1] - width :]
    return jnp.concatenate(
        [
            lax.ppermute(tail, "band", [(i, (i + 1) % count) for i in range(ends)]),
            cells,
            lax.ppermute(head, "band", [((i + 1) % count, i) for i in range(ends)]),
        ],
        axis=1,
    )


def masked_weights(responses, tap_counts, panel_links, first_tap):
    tap_dev, coupled_ports, group_ports = responses.shape
    half_width = (coupled_ports - group_ports) // 2
    tap_index = first_tap + jnp.arange(tap_dev, dtype=jnp.int32)
    tap_alive = tap_index[:, None] < tap_counts[None, :]
    port_index = jnp.arange(coupled_ports, dtype=jnp.int32)[:, None]
    lower_open = panel_links[None, :, 0] == 1
    upper_open = panel_links[None, :, 1] == 1
    couple_open = jnp.where(
        port_index < half_width,
        lower_open,
        jnp.where(port_index >= half_width + group_ports, upper_open, True),
    )
    keep_mask = tap_alive[:, None, :] & couple_open[None, :, :]
    return jnp.where(keep_mask, responses, jnp.zeros_like(responses))


def swap_core(x):
    return lax.ppermute(x, "core", [(0, 1), (1, 0)])


def band_halo(cells, width):
    count = lax.axis_size("band")
    ends = count - 1
    head = cells[..., :width]
    tail = cells[..., cells.shape[-1] - width :]
    below = lax.ppermute(tail, "band", [(i, (i + 1) % count) for i in range(ends)])
    above = lax.ppermute(head, "band", [((i + 1) % count, i) for i in range(ends)])
    return jnp.concatenate([below, above], axis=-1)


def assemble(needed, base, first_pair, pair_rows, length, other=None):
    if other is None:
        other = swap_core(needed)
    first = lax.axis_index("core") == 0
    pair = jnp.stack([jnp.where(first, needed, other), jnp.where(first, other, needed)], 1)
    rows = pair.reshape(-1, needed.shape[-1])
    return lax.dynamic_slice_in_dim(rows, base - first_pair * pair_rows, length, 0)


def split_windows(x, base, length, align, width):
    chips = lax.axis_size("y") * lax.axis_size("zh")
    spread = jnp.broadcast_to(x[None], (chips,) + x.shape)
    mine = lax.all_to_all(spread, ("y", "zh"), 0, 0, tiled=True)
    pair_rows = 2 * x.shape[0]
    span = (length + 2 * pair_rows - align - 1) // pair_rows
    first_pair = jnp.minimum(base // pair_rows, chips - span)
    needed = lax.dynamic_slice_in_dim(mine, first_pair, span, 0)
    edges = band_halo(needed, width)
    own = assemble(needed, base, first_pair, pair_rows, length)
    return own, lambda edges, other: assemble(edges, base, first_pair, pair_rows, length, other), edges


def reduce_scatter(partial, n_tm):
    chips = n_tm // 2
    blocks = partial.reshape(chips, 2, partial.shape[0] // n_tm, partial.shape[1])
    first = lax.axis_index("core") == 0
    keep = jnp.where(first, blocks[:, 0], blocks[:, 1])
    give = jnp.where(first, blocks[:, 1], blocks[:, 0])
    combined = keep + swap_core(give)
    return lax.all_to_all(combined, ("y", "zh"), 0, 0, tiled=True).sum(0)


def tm_index():
    return (lax.axis_index("y") * lax.axis_size("zh") + lax.axis_index("zh")) * lax.axis_size(
        "core"
    ) + lax.axis_index("core")


ROW_TILE = 512


def conv_kernel(segments, x_ref, w_ref, m_ref, *refs):
    if len(refs) == 3:
        acc_ref, o_ref, wm_ref = refs
    else:
        acc_ref = None
        o_ref, wm_ref = refs
    taps = w_ref.shape[0]
    ports = o_ref.shape[1]
    for k in range(taps):
        marks = m_ref[k]
        for lo, hi, row, at in segments:
            keep = marks[row : row + 1, :] != 0
            block = w_ref[k, lo:hi, :]
            wm_ref[k, at : at + hi - lo, :] = jnp.where(keep, block, jnp.zeros_like(block))
    rows = o_ref.shape[0]
    for r in range(rows // ROW_TILE):
        start = r * ROW_TILE
        if acc_ref is None:
            acc = jnp.zeros((ROW_TILE, ports), jnp.float32)
        else:
            acc = acc_ref[start : start + ROW_TILE, :]
        for k in range(taps):
            shift = taps - k
            acc = acc + jnp.dot(
                x_ref[start + shift : start + shift + ROW_TILE, :],
                wm_ref[k],
                preferred_element_type=jnp.float32,
            )
        o_ref[start : start + ROW_TILE, :] = acc


def conv_part(window, responses, marks, rows, segments, acc=None):
    taps, coupled, ports = responses.shape
    depth = window.shape[1]
    vmem = pl.BlockSpec(memory_space=pltpu.VMEM)
    operands = [window, responses, marks] + ([] if acc is None else [acc])
    return pl.pallas_call(
        functools.partial(conv_kernel, segments),
        out_shape=jax.ShapeDtypeStruct((rows, ports), jnp.float32),
        in_specs=[vmem] * len(operands),
        out_specs=vmem,
        scratch_shapes=[pltpu.VMEM((taps, depth, ports), responses.dtype)],
        input_output_aliases={} if acc is None else {3: 0},
        compiler_params=pltpu.CompilerParams(vmem_limit_bytes=48 * 1024 * 1024),
        cost_estimate=pl.CostEstimate(
            flops=2 * rows * taps * depth * ports,
            transcendentals=0,
            bytes_accessed=window.size * 2 + taps * depth * ports * 2 + rows * ports * 4,
        ),
    )(*operands)


def tap_marks(tap_counts, panel_links, first_tap, taps):
    tap_index = first_tap + jnp.arange(taps, dtype=jnp.int32)
    alive = tap_index[:, None] < tap_counts[None, :]
    lower = alive & (panel_links[None, :, 0] == 1)
    upper = alive & (panel_links[None, :, 1] == 1)
    marks = jnp.stack([lower, alive, upper], 1).astype(jnp.int32)
    return jnp.pad(marks, ((0, 0), (0, 5), (0, 0)))


def per_device(driven_wave, responses, tap_counts, panel_links):
    tap_dev = responses.shape[0]
    group_ports = driven_wave.shape[1]
    half_width = group_ports // 2
    n_tm = lax.axis_size("y") * lax.axis_size("zh") * lax.axis_size("core")
    total_taps = tap_dev * n_tm
    window_len = driven_wave.shape[0] * n_tm - total_taps
    me = tm_index()
    first_tap = me * tap_dev
    base = total_taps - first_tap - tap_dev
    own, halo_of, edges = split_windows(driven_wave, base, window_len + tap_dev, tap_dev, half_width)
    marks = tap_marks(tap_counts, panel_links, first_tap, tap_dev)
    ports = group_ports
    partial = conv_part(own, responses, marks, window_len, ((half_width, half_width + ports, 1, 0),))
    other_edges = swap_core(edges)
    partial, edges, other_edges = lax.optimization_barrier((partial, edges, other_edges))
    partial = conv_part(
        halo_of(edges, other_edges),
        responses,
        marks,
        window_len,
        ((0, half_width, 0, 0), (half_width + ports, 2 * ports, 2, half_width)),
        partial,
    )
    summed = reduce_scatter(partial, n_tm)
    return summed.astype(jnp.bfloat16)


def solution(mesh):
    band, tm = mesh.devices.shape
    view = Mesh(mesh.devices.reshape(band, tm // 8, 4, 2), ("band",) + TM)
    return jax.shard_map(
        per_device,
        mesh=view,
        in_specs=(P(TM, "band"), P(TM, None, "band"), P("band"), P("band", None)),
        out_specs=P(TM, "band"),
        check_vma=False,
    )
```

```python
import functools

import jax
import jax.numpy as jnp
from jax import lax
from jax.experimental import pallas as pl
from jax.experimental.pallas import tpu as pltpu
from jax.sharding import Mesh
from jax.sharding import PartitionSpec as P

TM = ("y", "zh", "core")


def extended(cells, width):
    count = lax.axis_size("band")
    ends = count - 1
    head = cells[:, :width]
    tail = cells[:, cells.shape[1] - width :]
    return jnp.concatenate(
        [
            lax.ppermute(tail, "band", [(i, (i + 1) % count) for i in range(ends)]),
            cells,
            lax.ppermute(head, "band", [((i + 1) % count, i) for i in range(ends)]),
        ],
        axis=1,
    )


def masked_weights(responses, tap_counts, panel_links, first_tap):
    tap_dev, coupled_ports, group_ports = responses.shape
    half_width = (coupled_ports - group_ports) // 2
    tap_index = first_tap + jnp.arange(tap_dev, dtype=jnp.int32)
    tap_alive = tap_index[:, None] < tap_counts[None, :]
    port_index = jnp.arange(coupled_ports, dtype=jnp.int32)[:, None]
    lower_open = panel_links[None, :, 0] == 1
    upper_open = panel_links[None, :, 1] == 1
    couple_open = jnp.where(
        port_index < half_width,
        lower_open,
        jnp.where(port_index >= half_width + group_ports, upper_open, True),
    )
    keep_mask = tap_alive[:, None, :] & couple_open[None, :, :]
    return jnp.where(keep_mask, responses, jnp.zeros_like(responses))


def swap_core(x):
    return lax.ppermute(x, "core", [(0, 1), (1, 0)])


def band_halo(cells, width):
    count = lax.axis_size("band")
    ends = count - 1
    head = cells[..., :width]
    tail = cells[..., cells.shape[-1] - width :]
    below = lax.ppermute(tail, "band", [(i, (i + 1) % count) for i in range(ends)])
    above = lax.ppermute(head, "band", [((i + 1) % count, i) for i in range(ends)])
    return jnp.concatenate([below, above], axis=-1)


def assemble(needed, base, first_pair, pair_rows, length, other=None):
    if other is None:
        other = swap_core(needed)
    first = lax.axis_index("core") == 0
    pair = jnp.stack([jnp.where(first, needed, other), jnp.where(first, other, needed)], 1)
    rows = pair.reshape(-1, needed.shape[-1])
    return lax.dynamic_slice_in_dim(rows, base - first_pair * pair_rows, length, 0)


def split_windows(x, base, length, align, width):
    chips = lax.axis_size("y") * lax.axis_size("zh")
    spread = jnp.broadcast_to(x[None], (chips,) + x.shape)
    mine = lax.all_to_all(spread, ("y", "zh"), 0, 0, tiled=True)
    pair_rows = 2 * x.shape[0]
    span = (length + 2 * pair_rows - align - 1) // pair_rows
    first_pair = jnp.minimum(base // pair_rows, chips - span)
    needed = lax.dynamic_slice_in_dim(mine, first_pair, span, 0)
    edges = band_halo(needed, width)
    own = assemble(needed, base, first_pair, pair_rows, length)
    return own, lambda edges, other: assemble(edges, base, first_pair, pair_rows, length, other), edges


def core_combine(partial, rows_per):
    blocks = partial.reshape(-1, 2, rows_per, partial.shape[1])
    first = lax.axis_index("core") == 0
    keep = jnp.where(first, blocks[:, 0], blocks[:, 1])
    give = jnp.where(first, blocks[:, 1], blocks[:, 0])
    return keep + swap_core(give)


def reduce_scatter(combined):
    return lax.all_to_all(combined, ("y", "zh"), 0, 0, tiled=True).sum(0)


def tm_index():
    return (lax.axis_index("y") * lax.axis_size("zh") + lax.axis_index("zh")) * lax.axis_size(
        "core"
    ) + lax.axis_index("core")


ROW_TILE = 512


def conv_kernel(segments, x_ref, w_ref, m_ref, *refs):
    if len(refs) == 3:
        acc_ref, o_ref, wm_ref = refs
    else:
        acc_ref = None
        o_ref, wm_ref = refs
    taps = w_ref.shape[0]
    ports = o_ref.shape[1]
    for k in range(taps):
        marks = m_ref[k]
        for lo, hi, row, at in segments:
            keep = marks[row : row + 1, :] != 0
            block = w_ref[k, lo:hi, :]
            wm_ref[k, at : at + hi - lo, :] = jnp.where(keep, block, jnp.zeros_like(block))
    rows = o_ref.shape[0]
    for r in range(rows // ROW_TILE):
        start = r * ROW_TILE
        if acc_ref is None:
            acc = jnp.zeros((ROW_TILE, ports), jnp.float32)
        else:
            acc = acc_ref[start : start + ROW_TILE, :]
        for k in range(taps):
            shift = taps - k
            acc = acc + jnp.dot(
                x_ref[start + shift : start + shift + ROW_TILE, :],
                wm_ref[k],
                preferred_element_type=jnp.float32,
            )
        o_ref[start : start + ROW_TILE, :] = acc


def conv_part(window, responses, marks, rows, segments, acc=None):
    taps, coupled, ports = responses.shape
    depth = window.shape[1]
    vmem = pl.BlockSpec(memory_space=pltpu.VMEM)
    operands = [window, responses, marks] + ([] if acc is None else [acc])
    return pl.pallas_call(
        functools.partial(conv_kernel, segments),
        out_shape=jax.ShapeDtypeStruct((rows, ports), jnp.float32),
        in_specs=[vmem] * len(operands),
        out_specs=vmem,
        scratch_shapes=[pltpu.VMEM((taps, depth, ports), responses.dtype)],
        input_output_aliases={} if acc is None else {3: 0},
        compiler_params=pltpu.CompilerParams(vmem_limit_bytes=48 * 1024 * 1024),
        cost_estimate=pl.CostEstimate(
            flops=2 * rows * taps * depth * ports,
            transcendentals=0,
            bytes_accessed=window.size * 2 + taps * depth * ports * 2 + rows * ports * 4,
        ),
    )(*operands)


def tap_marks(tap_counts, panel_links, first_tap, taps):
    tap_index = first_tap + jnp.arange(taps, dtype=jnp.int32)
    alive = tap_index[:, None] < tap_counts[None, :]
    lower = alive & (panel_links[None, :, 0] == 1)
    upper = alive & (panel_links[None, :, 1] == 1)
    marks = jnp.stack([lower, alive, upper], 1).astype(jnp.int32)
    return jnp.pad(marks, ((0, 0), (0, 5), (0, 0)))


def per_device(driven_wave, responses, tap_counts, panel_links):
    tap_dev = responses.shape[0]
    group_ports = driven_wave.shape[1]
    half_width = group_ports // 2
    n_tm = lax.axis_size("y") * lax.axis_size("zh") * lax.axis_size("core")
    total_taps = tap_dev * n_tm
    window_len = driven_wave.shape[0] * n_tm - total_taps
    me = tm_index()
    first_tap = me * tap_dev
    base = total_taps - first_tap - tap_dev
    own, halo_of, edges = split_windows(driven_wave, base, window_len + tap_dev, tap_dev, half_width)
    marks = tap_marks(tap_counts, panel_links, first_tap, tap_dev)
    ports = group_ports
    partial = conv_part(own, responses, marks, window_len, ((half_width, half_width + ports, 1, 0),))
    other_edges = swap_core(edges)
    partial, edges, other_edges = lax.optimization_barrier((partial, edges, other_edges))
    halo = halo_of(edges, other_edges)
    half = window_len // 2
    segments = ((0, half_width, 0, 0), (half_width + ports, 2 * ports, 2, half_width))
    rows_per = window_len // n_tm
    first_half = conv_part(halo[: half + tap_dev], responses, marks, half, segments, partial[:half])
    combined_first = core_combine(first_half, rows_per)
    second_half = conv_part(halo[half:], responses, marks, half, segments, partial[half:])
    combined = jnp.concatenate([combined_first, core_combine(second_half, rows_per)], 0)
    summed = reduce_scatter(combined)
    return summed.astype(jnp.bfloat16)


def solution(mesh):
    band, tm = mesh.devices.shape
    view = Mesh(mesh.devices.reshape(band, tm // 8, 4, 2), ("band",) + TM)
    return jax.shard_map(
        per_device,
        mesh=view,
        in_specs=(P(TM, "band"), P(TM, None, "band"), P("band"), P("band", None)),
        out_specs=P(TM, "band"),
        check_vma=False,
    )
```

```python
import functools

import jax
import jax.numpy as jnp
from jax import lax
from jax.experimental import pallas as pl
from jax.experimental.pallas import tpu as pltpu
from jax.sharding import Mesh
from jax.sharding import PartitionSpec as P

TM = ("y", "zh", "core")


def extended(cells, width):
    count = lax.axis_size("band")
    ends = count - 1
    head = cells[:, :width]
    tail = cells[:, cells.shape[1] - width :]
    return jnp.concatenate(
        [
            lax.ppermute(tail, "band", [(i, (i + 1) % count) for i in range(ends)]),
            cells,
            lax.ppermute(head, "band", [((i + 1) % count, i) for i in range(ends)]),
        ],
        axis=1,
    )


def masked_weights(responses, tap_counts, panel_links, first_tap):
    tap_dev, coupled_ports, group_ports = responses.shape
    half_width = (coupled_ports - group_ports) // 2
    tap_index = first_tap + jnp.arange(tap_dev, dtype=jnp.int32)
    tap_alive = tap_index[:, None] < tap_counts[None, :]
    port_index = jnp.arange(coupled_ports, dtype=jnp.int32)[:, None]
    lower_open = panel_links[None, :, 0] == 1
    upper_open = panel_links[None, :, 1] == 1
    couple_open = jnp.where(
        port_index < half_width,
        lower_open,
        jnp.where(port_index >= half_width + group_ports, upper_open, True),
    )
    keep_mask = tap_alive[:, None, :] & couple_open[None, :, :]
    return jnp.where(keep_mask, responses, jnp.zeros_like(responses))


def swap_core(x):
    return lax.ppermute(x, "core", [(0, 1), (1, 0)])


def band_halo(cells, width):
    count = lax.axis_size("band")
    ends = count - 1
    head = cells[..., :width]
    tail = cells[..., cells.shape[-1] - width :]
    below = lax.ppermute(tail, "band", [(i, (i + 1) % count) for i in range(ends)])
    above = lax.ppermute(head, "band", [((i + 1) % count, i) for i in range(ends)])
    return jnp.concatenate([below, above], axis=-1)


def assemble(needed, base, first_pair, pair_rows, length, other=None):
    if other is None:
        other = swap_core(needed)
    first = lax.axis_index("core") == 0
    pair = jnp.stack([jnp.where(first, needed, other), jnp.where(first, other, needed)], 1)
    rows = pair.reshape(-1, needed.shape[-1])
    return lax.dynamic_slice_in_dim(rows, base - first_pair * pair_rows, length, 0)


def split_windows(x, base, length, align, width):
    chips = lax.axis_size("y") * lax.axis_size("zh")
    spread = jnp.broadcast_to(x[None], (chips,) + x.shape)
    mine = lax.all_to_all(spread, ("y", "zh"), 0, 0, tiled=True)
    pair_rows = 2 * x.shape[0]
    span = (length + 2 * pair_rows - align - 1) // pair_rows
    first_pair = jnp.minimum(base // pair_rows, chips - span)
    needed = lax.dynamic_slice_in_dim(mine, first_pair, span, 0)
    other = swap_core(needed)
    first = lax.axis_index("core") == 0
    pair = jnp.stack([jnp.where(first, needed, other), jnp.where(first, other, needed)], 1)
    rows = pair.reshape(-1, needed.shape[-1])
    offset = base - first_pair * pair_rows
    own = lax.dynamic_slice_in_dim(rows, offset, length, 0)
    edges = band_halo(rows, width)
    return own, lambda edges: lax.dynamic_slice_in_dim(edges, offset, length, 0), edges


def reduce_scatter(partial, n_tm):
    chips = n_tm // 2
    blocks = partial.reshape(chips, 2, partial.shape[0] // n_tm, partial.shape[1])
    first = lax.axis_index("core") == 0
    keep = jnp.where(first, blocks[:, 0], blocks[:, 1])
    give = jnp.where(first, blocks[:, 1], blocks[:, 0])
    combined = keep + swap_core(give)
    return lax.all_to_all(combined, ("y", "zh"), 0, 0, tiled=True).sum(0)


def tm_index():
    return (lax.axis_index("y") * lax.axis_size("zh") + lax.axis_index("zh")) * lax.axis_size(
        "core"
    ) + lax.axis_index("core")


ROW_TILE = 512


def conv_kernel(segments, x_ref, w_ref, m_ref, *refs):
    if len(refs) == 3:
        acc_ref, o_ref, wm_ref = refs
    else:
        acc_ref = None
        o_ref, wm_ref = refs
    taps = w_ref.shape[0]
    ports = o_ref.shape[1]
    for k in range(taps):
        marks = m_ref[k]
        for lo, hi, row, at in segments:
            keep = marks[row : row + 1, :] != 0
            block = w_ref[k, lo:hi, :]
            wm_ref[k, at : at + hi - lo, :] = jnp.where(keep, block, jnp.zeros_like(block))
    rows = o_ref.shape[0]
    for r in range(rows // ROW_TILE):
        start = r * ROW_TILE
        if acc_ref is None:
            acc = jnp.zeros((ROW_TILE, ports), jnp.float32)
        else:
            acc = acc_ref[start : start + ROW_TILE, :]
        for k in range(taps):
            shift = taps - k
            acc = acc + jnp.dot(
                x_ref[start + shift : start + shift + ROW_TILE, :],
                wm_ref[k],
                preferred_element_type=jnp.float32,
            )
        o_ref[start : start + ROW_TILE, :] = acc


def conv_part(window, responses, marks, rows, segments, acc=None):
    taps, coupled, ports = responses.shape
    depth = window.shape[1]
    vmem = pl.BlockSpec(memory_space=pltpu.VMEM)
    operands = [window, responses, marks] + ([] if acc is None else [acc])
    return pl.pallas_call(
        functools.partial(conv_kernel, segments),
        out_shape=jax.ShapeDtypeStruct((rows, ports), jnp.float32),
        in_specs=[vmem] * len(operands),
        out_specs=vmem,
        scratch_shapes=[pltpu.VMEM((taps, depth, ports), responses.dtype)],
        input_output_aliases={} if acc is None else {3: 0},
        compiler_params=pltpu.CompilerParams(vmem_limit_bytes=48 * 1024 * 1024),
        cost_estimate=pl.CostEstimate(
            flops=2 * rows * taps * depth * ports,
            transcendentals=0,
            bytes_accessed=window.size * 2 + taps * depth * ports * 2 + rows * ports * 4,
        ),
    )(*operands)


def tap_marks(tap_counts, panel_links, first_tap, taps):
    tap_index = first_tap + jnp.arange(taps, dtype=jnp.int32)
    alive = tap_index[:, None] < tap_counts[None, :]
    lower = alive & (panel_links[None, :, 0] == 1)
    upper = alive & (panel_links[None, :, 1] == 1)
    marks = jnp.stack([lower, alive, upper], 1).astype(jnp.int32)
    return jnp.pad(marks, ((0, 0), (0, 5), (0, 0)))


def per_device(driven_wave, responses, tap_counts, panel_links):
    tap_dev = responses.shape[0]
    group_ports = driven_wave.shape[1]
    half_width = group_ports // 2
    n_tm = lax.axis_size("y") * lax.axis_size("zh") * lax.axis_size("core")
    total_taps = tap_dev * n_tm
    window_len = driven_wave.shape[0] * n_tm - total_taps
    me = tm_index()
    first_tap = me * tap_dev
    base = total_taps - first_tap - tap_dev
    own, halo_of, edges = split_windows(driven_wave, base, window_len + tap_dev, tap_dev, half_width)
    marks = tap_marks(tap_counts, panel_links, first_tap, tap_dev)
    ports = group_ports
    partial = conv_part(own, responses, marks, window_len, ((half_width, half_width + ports, 1, 0),))
    partial, edges = lax.optimization_barrier((partial, edges))
    partial = conv_part(
        halo_of(edges),
        responses,
        marks,
        window_len,
        ((0, half_width, 0, 0), (half_width + ports, 2 * ports, 2, half_width)),
        partial,
    )
    summed = reduce_scatter(partial, n_tm)
    return summed.astype(jnp.bfloat16)


def solution(mesh):
    band, tm = mesh.devices.shape
    view = Mesh(mesh.devices.reshape(band, tm // 8, 4, 2), ("band",) + TM)
    return jax.shard_map(
        per_device,
        mesh=view,
        in_specs=(P(TM, "band"), P(TM, None, "band"), P("band"), P("band", None)),
        out_specs=P(TM, "band"),
        check_vma=False,
    )
```

```python
import functools

import jax
import jax.numpy as jnp
from jax import lax
from jax.experimental import pallas as pl
from jax.experimental.pallas import tpu as pltpu
from jax.sharding import Mesh
from jax.sharding import PartitionSpec as P

TM = ("y", "zh", "core")


def extended(cells, width):
    count = lax.axis_size("band")
    ends = count - 1
    head = cells[:, :width]
    tail = cells[:, cells.shape[1] - width :]
    return jnp.concatenate(
        [
            lax.ppermute(tail, "band", [(i, (i + 1) % count) for i in range(ends)]),
            cells,
            lax.ppermute(head, "band", [((i + 1) % count, i) for i in range(ends)]),
        ],
        axis=1,
    )


def masked_weights(responses, tap_counts, panel_links, first_tap):
    tap_dev, coupled_ports, group_ports = responses.shape
    half_width = (coupled_ports - group_ports) // 2
    tap_index = first_tap + jnp.arange(tap_dev, dtype=jnp.int32)
    tap_alive = tap_index[:, None] < tap_counts[None, :]
    port_index = jnp.arange(coupled_ports, dtype=jnp.int32)[:, None]
    lower_open = panel_links[None, :, 0] == 1
    upper_open = panel_links[None, :, 1] == 1
    couple_open = jnp.where(
        port_index < half_width,
        lower_open,
        jnp.where(port_index >= half_width + group_ports, upper_open, True),
    )
    keep_mask = tap_alive[:, None, :] & couple_open[None, :, :]
    return jnp.where(keep_mask, responses, jnp.zeros_like(responses))


def swap_core(x):
    return lax.ppermute(x, "core", [(0, 1), (1, 0)])


def band_halo(cells, width):
    count = lax.axis_size("band")
    ends = count - 1
    head = cells[..., :width]
    tail = cells[..., cells.shape[-1] - width :]
    below = lax.ppermute(tail, "band", [(i, (i + 1) % count) for i in range(ends)])
    above = lax.ppermute(head, "band", [((i + 1) % count, i) for i in range(ends)])
    return jnp.concatenate([below, above], axis=-1)


def assemble(needed, base, first_pair, pair_rows, length, other=None):
    if other is None:
        other = swap_core(needed)
    first = lax.axis_index("core") == 0
    pair = jnp.stack([jnp.where(first, needed, other), jnp.where(first, other, needed)], 1)
    rows = pair.reshape(-1, needed.shape[-1])
    return lax.dynamic_slice_in_dim(rows, base - first_pair * pair_rows, length, 0)


def split_windows(x, base, length, align, width):
    chips = lax.axis_size("y") * lax.axis_size("zh")
    spread = jnp.broadcast_to(x[None], (chips,) + x.shape)
    mine = lax.all_to_all(spread, ("y", "zh"), 0, 0, tiled=True)
    pair_rows = 2 * x.shape[0]
    span = (length + 2 * pair_rows - align - 1) // pair_rows
    first_pair = jnp.minimum(base // pair_rows, chips - span)
    needed = lax.dynamic_slice_in_dim(mine, first_pair, span, 0)
    edges = band_halo(needed, width)
    own = assemble(needed, base, first_pair, pair_rows, length)
    return own, lambda edges, other: assemble(edges, base, first_pair, pair_rows, length, other), edges


def reduce_scatter(partial, n_tm):
    chips = n_tm // 2
    blocks = partial.reshape(chips, 2, partial.shape[0] // n_tm, partial.shape[1])
    first = lax.axis_index("core") == 0
    keep = jnp.where(first, blocks[:, 0], blocks[:, 1])
    give = jnp.where(first, blocks[:, 1], blocks[:, 0])
    combined = keep + swap_core(give)
    return lax.all_to_all(combined, ("y", "zh"), 0, 0, tiled=True).sum(0)


def tm_index():
    return (lax.axis_index("y") * lax.axis_size("zh") + lax.axis_index("zh")) * lax.axis_size(
        "core"
    ) + lax.axis_index("core")


ROW_TILE = 256


def conv_kernel(segments, x_ref, w_ref, m_ref, *refs):
    if len(refs) == 3:
        acc_ref, o_ref, wm_ref = refs
    else:
        acc_ref = None
        o_ref, wm_ref = refs
    taps = w_ref.shape[0]
    ports = o_ref.shape[1]
    for k in range(taps):
        marks = m_ref[k]
        for lo, hi, row, at in segments:
            keep = marks[row : row + 1, :] != 0
            block = w_ref[k, lo:hi, :]
            wm_ref[k, at : at + hi - lo, :] = jnp.where(keep, block, jnp.zeros_like(block))
    rows = o_ref.shape[0]
    for r in range(rows // ROW_TILE):
        start = r * ROW_TILE
        if acc_ref is None:
            acc = jnp.zeros((ROW_TILE, ports), jnp.float32)
        else:
            acc = acc_ref[start : start + ROW_TILE, :]
        for k in range(taps):
            shift = taps - k
            acc = acc + jnp.dot(
                x_ref[start + shift : start + shift + ROW_TILE, :],
                wm_ref[k],
                preferred_element_type=jnp.float32,
            )
        o_ref[start : start + ROW_TILE, :] = acc


def conv_part(window, responses, marks, rows, segments, acc=None):
    taps, coupled, ports = responses.shape
    depth = window.shape[1]
    vmem = pl.BlockSpec(memory_space=pltpu.VMEM)
    operands = [window, responses, marks] + ([] if acc is None else [acc])
    return pl.pallas_call(
        functools.partial(conv_kernel, segments),
        out_shape=jax.ShapeDtypeStruct((rows, ports), jnp.float32),
        in_specs=[vmem] * len(operands),
        out_specs=vmem,
        scratch_shapes=[pltpu.VMEM((taps, depth, ports), responses.dtype)],
        input_output_aliases={} if acc is None else {3: 0},
        compiler_params=pltpu.CompilerParams(vmem_limit_bytes=48 * 1024 * 1024),
        cost_estimate=pl.CostEstimate(
            flops=2 * rows * taps * depth * ports,
            transcendentals=0,
            bytes_accessed=window.size * 2 + taps * depth * ports * 2 + rows * ports * 4,
        ),
    )(*operands)


def tap_marks(tap_counts, panel_links, first_tap, taps):
    tap_index = first_tap + jnp.arange(taps, dtype=jnp.int32)
    alive = tap_index[:, None] < tap_counts[None, :]
    lower = alive & (panel_links[None, :, 0] == 1)
    upper = alive & (panel_links[None, :, 1] == 1)
    marks = jnp.stack([lower, alive, upper], 1).astype(jnp.int32)
    return jnp.pad(marks, ((0, 0), (0, 5), (0, 0)))


def per_device(driven_wave, responses, tap_counts, panel_links):
    tap_dev = responses.shape[0]
    group_ports = driven_wave.shape[1]
    half_width = group_ports // 2
    n_tm = lax.axis_size("y") * lax.axis_size("zh") * lax.axis_size("core")
    total_taps = tap_dev * n_tm
    window_len = driven_wave.shape[0] * n_tm - total_taps
    me = tm_index()
    first_tap = me * tap_dev
    base = total_taps - first_tap - tap_dev
    own, halo_of, edges = split_windows(driven_wave, base, window_len + tap_dev, tap_dev, half_width)
    marks = tap_marks(tap_counts, panel_links, first_tap, tap_dev)
    ports = group_ports
    partial = conv_part(own, responses, marks, window_len, ((half_width, half_width + ports, 1, 0),))
    other_edges = swap_core(edges)
    partial, edges, other_edges = lax.optimization_barrier((partial, edges, other_edges))
    partial = conv_part(
        halo_of(edges, other_edges),
        responses,
        marks,
        window_len,
        ((0, half_width, 0, 0), (half_width + ports, 2 * ports, 2, half_width)),
        partial,
    )
    summed = reduce_scatter(partial, n_tm)
    return summed.astype(jnp.bfloat16)


def solution(mesh):
    band, tm = mesh.devices.shape
    view = Mesh(mesh.devices.reshape(band, tm // 8, 4, 2), ("band",) + TM)
    return jax.shard_map(
        per_device,
        mesh=view,
        in_specs=(P(TM, "band"), P(TM, None, "band"), P("band"), P("band", None)),
        out_specs=P(TM, "band"),
        check_vma=False,
    )
```

```python
import functools

import jax
import jax.numpy as jnp
from jax import lax
from jax.experimental import pallas as pl
from jax.experimental.pallas import tpu as pltpu
from jax.sharding import Mesh
from jax.sharding import PartitionSpec as P

TM = ("y", "zh", "core")


def extended(cells, width):
    count = lax.axis_size("band")
    ends = count - 1
    head = cells[:, :width]
    tail = cells[:, cells.shape[1] - width :]
    return jnp.concatenate(
        [
            lax.ppermute(tail, "band", [(i, (i + 1) % count) for i in range(ends)]),
            cells,
            lax.ppermute(head, "band", [((i + 1) % count, i) for i in range(ends)]),
        ],
        axis=1,
    )


def masked_weights(responses, tap_counts, panel_links, first_tap):
    tap_dev, coupled_ports, group_ports = responses.shape
    half_width = (coupled_ports - group_ports) // 2
    tap_index = first_tap + jnp.arange(tap_dev, dtype=jnp.int32)
    tap_alive = tap_index[:, None] < tap_counts[None, :]
    port_index = jnp.arange(coupled_ports, dtype=jnp.int32)[:, None]
    lower_open = panel_links[None, :, 0] == 1
    upper_open = panel_links[None, :, 1] == 1
    couple_open = jnp.where(
        port_index < half_width,
        lower_open,
        jnp.where(port_index >= half_width + group_ports, upper_open, True),
    )
    keep_mask = tap_alive[:, None, :] & couple_open[None, :, :]
    return jnp.where(keep_mask, responses, jnp.zeros_like(responses))


def swap_core(x):
    return lax.ppermute(x, "core", [(0, 1), (1, 0)])


def band_halo(cells, width):
    count = lax.axis_size("band")
    ends = count - 1
    head = cells[..., :width]
    tail = cells[..., cells.shape[-1] - width :]
    below = lax.ppermute(tail, "band", [(i, (i + 1) % count) for i in range(ends)])
    above = lax.ppermute(head, "band", [((i + 1) % count, i) for i in range(ends)])
    return jnp.concatenate([below, above], axis=-1)


def assemble(needed, base, first_pair, pair_rows, length, other=None):
    if other is None:
        other = swap_core(needed)
    first = lax.axis_index("core") == 0
    pair = jnp.stack([jnp.where(first, needed, other), jnp.where(first, other, needed)], 1)
    rows = pair.reshape(-1, needed.shape[-1])
    return lax.dynamic_slice_in_dim(rows, base - first_pair * pair_rows, length, 0)


def split_windows(x, base, length, align, width):
    chips = lax.axis_size("y") * lax.axis_size("zh")
    spread = jnp.broadcast_to(x[None], (chips,) + x.shape)
    mine = lax.all_to_all(spread, ("y", "zh"), 0, 0, tiled=True)
    pair_rows = 2 * x.shape[0]
    span = (length + 2 * pair_rows - align - 1) // pair_rows
    first_pair = jnp.minimum(base // pair_rows, chips - span)
    needed = lax.dynamic_slice_in_dim(mine, first_pair, span, 0)
    edges = band_halo(needed, width)
    own = assemble(needed, base, first_pair, pair_rows, length)
    return own, lambda edges, other: assemble(edges, base, first_pair, pair_rows, length, other), edges


def sum_kernel(x_ref, o_ref):
    acc = x_ref[0]
    for c in range(1, x_ref.shape[0]):
        acc = acc + x_ref[c]
    o_ref[...] = acc.astype(o_ref.dtype)


def sum_blocks(blocks):
    vmem = pl.BlockSpec(memory_space=pltpu.VMEM)
    return pl.pallas_call(
        sum_kernel,
        out_shape=jax.ShapeDtypeStruct(blocks.shape[1:], jnp.bfloat16),
        in_specs=[vmem],
        out_specs=vmem,
    )(blocks)


def reduce_scatter(partial, n_tm):
    chips = n_tm // 2
    blocks = partial.reshape(chips, 2, partial.shape[0] // n_tm, partial.shape[1])
    first = lax.axis_index("core") == 0
    keep = jnp.where(first, blocks[:, 0], blocks[:, 1])
    give = jnp.where(first, blocks[:, 1], blocks[:, 0])
    combined = keep + swap_core(give)
    return sum_blocks(lax.all_to_all(combined, ("y", "zh"), 0, 0, tiled=True))


def tm_index():
    return (lax.axis_index("y") * lax.axis_size("zh") + lax.axis_index("zh")) * lax.axis_size(
        "core"
    ) + lax.axis_index("core")


ROW_TILE = 256


def conv_kernel(segments, x_ref, w_ref, m_ref, *refs):
    if len(refs) == 3:
        acc_ref, o_ref, wm_ref = refs
    else:
        acc_ref = None
        o_ref, wm_ref = refs
    taps = w_ref.shape[0]
    ports = o_ref.shape[1]
    for k in range(taps):
        marks = m_ref[k]
        for lo, hi, row, at in segments:
            keep = marks[row : row + 1, :] != 0
            block = w_ref[k, lo:hi, :]
            wm_ref[k, at : at + hi - lo, :] = jnp.where(keep, block, jnp.zeros_like(block))
    rows = o_ref.shape[0]
    for r in range(rows // ROW_TILE):
        start = r * ROW_TILE
        if acc_ref is None:
            acc = jnp.zeros((ROW_TILE, ports), jnp.float32)
        else:
            acc = acc_ref[start : start + ROW_TILE, :]
        for k in range(taps):
            shift = taps - k
            acc = acc + jnp.dot(
                x_ref[start + shift : start + shift + ROW_TILE, :],
                wm_ref[k],
                preferred_element_type=jnp.float32,
            )
        o_ref[start : start + ROW_TILE, :] = acc


def conv_part(window, responses, marks, rows, segments, acc=None):
    taps, coupled, ports = responses.shape
    depth = window.shape[1]
    vmem = pl.BlockSpec(memory_space=pltpu.VMEM)
    operands = [window, responses, marks] + ([] if acc is None else [acc])
    return pl.pallas_call(
        functools.partial(conv_kernel, segments),
        out_shape=jax.ShapeDtypeStruct((rows, ports), jnp.float32),
        in_specs=[vmem] * len(operands),
        out_specs=vmem,
        scratch_shapes=[pltpu.VMEM((taps, depth, ports), responses.dtype)],
        input_output_aliases={} if acc is None else {3: 0},
        compiler_params=pltpu.CompilerParams(vmem_limit_bytes=48 * 1024 * 1024),
        cost_estimate=pl.CostEstimate(
            flops=2 * rows * taps * depth * ports,
            transcendentals=0,
            bytes_accessed=window.size * 2 + taps * depth * ports * 2 + rows * ports * 4,
        ),
    )(*operands)


def tap_marks(tap_counts, panel_links, first_tap, taps):
    tap_index = first_tap + jnp.arange(taps, dtype=jnp.int32)
    alive = tap_index[:, None] < tap_counts[None, :]
    lower = alive & (panel_links[None, :, 0] == 1)
    upper = alive & (panel_links[None, :, 1] == 1)
    marks = jnp.stack([lower, alive, upper], 1).astype(jnp.int32)
    return jnp.pad(marks, ((0, 0), (0, 5), (0, 0)))


def per_device(driven_wave, responses, tap_counts, panel_links):
    tap_dev = responses.shape[0]
    group_ports = driven_wave.shape[1]
    half_width = group_ports // 2
    n_tm = lax.axis_size("y") * lax.axis_size("zh") * lax.axis_size("core")
    total_taps = tap_dev * n_tm
    window_len = driven_wave.shape[0] * n_tm - total_taps
    me = tm_index()
    first_tap = me * tap_dev
    base = total_taps - first_tap - tap_dev
    own, halo_of, edges = split_windows(driven_wave, base, window_len + tap_dev, tap_dev, half_width)
    marks = tap_marks(tap_counts, panel_links, first_tap, tap_dev)
    ports = group_ports
    partial = conv_part(own, responses, marks, window_len, ((half_width, half_width + ports, 1, 0),))
    other_edges = swap_core(edges)
    partial, edges, other_edges = lax.optimization_barrier((partial, edges, other_edges))
    partial = conv_part(
        halo_of(edges, other_edges),
        responses,
        marks,
        window_len,
        ((0, half_width, 0, 0), (half_width + ports, 2 * ports, 2, half_width)),
        partial,
    )
    return reduce_scatter(partial, n_tm)


def solution(mesh):
    band, tm = mesh.devices.shape
    view = Mesh(mesh.devices.reshape(band, tm // 8, 4, 2), ("band",) + TM)
    return jax.shard_map(
        per_device,
        mesh=view,
        in_specs=(P(TM, "band"), P(TM, None, "band"), P("band"), P("band", None)),
        out_specs=P(TM, "band"),
        check_vma=False,
    )
```

```python
import functools

import jax
import jax.numpy as jnp
from jax import lax
from jax.experimental import pallas as pl
from jax.experimental.pallas import tpu as pltpu
from jax.sharding import Mesh
from jax.sharding import PartitionSpec as P

TM = ("y", "zh", "core")


def extended(cells, width):
    count = lax.axis_size("band")
    ends = count - 1
    head = cells[:, :width]
    tail = cells[:, cells.shape[1] - width :]
    return jnp.concatenate(
        [
            lax.ppermute(tail, "band", [(i, (i + 1) % count) for i in range(ends)]),
            cells,
            lax.ppermute(head, "band", [((i + 1) % count, i) for i in range(ends)]),
        ],
        axis=1,
    )


def masked_weights(responses, tap_counts, panel_links, first_tap):
    tap_dev, coupled_ports, group_ports = responses.shape
    half_width = (coupled_ports - group_ports) // 2
    tap_index = first_tap + jnp.arange(tap_dev, dtype=jnp.int32)
    tap_alive = tap_index[:, None] < tap_counts[None, :]
    port_index = jnp.arange(coupled_ports, dtype=jnp.int32)[:, None]
    lower_open = panel_links[None, :, 0] == 1
    upper_open = panel_links[None, :, 1] == 1
    couple_open = jnp.where(
        port_index < half_width,
        lower_open,
        jnp.where(port_index >= half_width + group_ports, upper_open, True),
    )
    keep_mask = tap_alive[:, None, :] & couple_open[None, :, :]
    return jnp.where(keep_mask, responses, jnp.zeros_like(responses))


def swap_core(x):
    return lax.ppermute(x, "core", [(0, 1), (1, 0)])


def band_halo(cells, width):
    count = lax.axis_size("band")
    ends = count - 1
    head = cells[..., :width]
    tail = cells[..., cells.shape[-1] - width :]
    below = lax.ppermute(tail, "band", [(i, (i + 1) % count) for i in range(ends)])
    above = lax.ppermute(head, "band", [((i + 1) % count, i) for i in range(ends)])
    return jnp.concatenate([below, above], axis=-1)


def assemble(needed, base, first_pair, pair_rows, length, other=None):
    if other is None:
        other = swap_core(needed)
    first = lax.axis_index("core") == 0
    pair = jnp.stack([jnp.where(first, needed, other), jnp.where(first, other, needed)], 1)
    rows = pair.reshape(-1, needed.shape[-1])
    return lax.dynamic_slice_in_dim(rows, base - first_pair * pair_rows, length, 0)


def split_windows(x, base, length, align, width):
    chips = lax.axis_size("y") * lax.axis_size("zh")
    spread = jnp.broadcast_to(x[None], (chips,) + x.shape)
    mine = lax.all_to_all(spread, ("y", "zh"), 0, 0, tiled=True)
    pair_rows = 2 * x.shape[0]
    span = (length + 2 * pair_rows - align - 1) // pair_rows
    first_pair = jnp.minimum(base // pair_rows, chips - span)
    needed = lax.dynamic_slice_in_dim(mine, first_pair, span, 0)
    needed, other = lax.optimization_barrier((needed, swap_core(needed)))
    edges = band_halo(needed, width)
    own = assemble(needed, base, first_pair, pair_rows, length, other)
    return own, lambda edges, other: assemble(edges, base, first_pair, pair_rows, length, other), edges


def reduce_scatter(partial, n_tm):
    chips = n_tm // 2
    blocks = partial.reshape(chips, 2, partial.shape[0] // n_tm, partial.shape[1])
    first = lax.axis_index("core") == 0
    keep = jnp.where(first, blocks[:, 0], blocks[:, 1])
    give = jnp.where(first, blocks[:, 1], blocks[:, 0])
    combined = keep + swap_core(give)
    return lax.all_to_all(combined, ("y", "zh"), 0, 0, tiled=True).sum(0)


def tm_index():
    return (lax.axis_index("y") * lax.axis_size("zh") + lax.axis_index("zh")) * lax.axis_size(
        "core"
    ) + lax.axis_index("core")


ROW_TILE = 256


def conv_kernel(segments, x_ref, w_ref, m_ref, *refs):
    if len(refs) == 3:
        acc_ref, o_ref, wm_ref = refs
    else:
        acc_ref = None
        o_ref, wm_ref = refs
    taps = w_ref.shape[0]
    ports = o_ref.shape[1]
    for k in range(taps):
        marks = m_ref[k]
        for lo, hi, row, at in segments:
            keep = marks[row : row + 1, :] != 0
            block = w_ref[k, lo:hi, :]
            wm_ref[k, at : at + hi - lo, :] = jnp.where(keep, block, jnp.zeros_like(block))
    rows = o_ref.shape[0]
    for r in range(rows // ROW_TILE):
        start = r * ROW_TILE
        if acc_ref is None:
            acc = jnp.zeros((ROW_TILE, ports), jnp.float32)
        else:
            acc = acc_ref[start : start + ROW_TILE, :]
        for k in range(taps):
            shift = taps - k
            acc = acc + jnp.dot(
                x_ref[start + shift : start + shift + ROW_TILE, :],
                wm_ref[k],
                preferred_element_type=jnp.float32,
            )
        o_ref[start : start + ROW_TILE, :] = acc


def conv_part(window, responses, marks, rows, segments, acc=None):
    taps, coupled, ports = responses.shape
    depth = window.shape[1]
    vmem = pl.BlockSpec(memory_space=pltpu.VMEM)
    operands = [window, responses, marks] + ([] if acc is None else [acc])
    return pl.pallas_call(
        functools.partial(conv_kernel, segments),
        out_shape=jax.ShapeDtypeStruct((rows, ports), jnp.float32),
        in_specs=[vmem] * len(operands),
        out_specs=vmem,
        scratch_shapes=[pltpu.VMEM((taps, depth, ports), responses.dtype)],
        input_output_aliases={} if acc is None else {3: 0},
        compiler_params=pltpu.CompilerParams(vmem_limit_bytes=48 * 1024 * 1024),
        cost_estimate=pl.CostEstimate(
            flops=2 * rows * taps * depth * ports,
            transcendentals=0,
            bytes_accessed=window.size * 2 + taps * depth * ports * 2 + rows * ports * 4,
        ),
    )(*operands)


def tap_marks(tap_counts, panel_links, first_tap, taps):
    tap_index = first_tap + jnp.arange(taps, dtype=jnp.int32)
    alive = tap_index[:, None] < tap_counts[None, :]
    lower = alive & (panel_links[None, :, 0] == 1)
    upper = alive & (panel_links[None, :, 1] == 1)
    marks = jnp.stack([lower, alive, upper], 1).astype(jnp.int32)
    return jnp.pad(marks, ((0, 0), (0, 5), (0, 0)))


def per_device(driven_wave, responses, tap_counts, panel_links):
    tap_dev = responses.shape[0]
    group_ports = driven_wave.shape[1]
    half_width = group_ports // 2
    n_tm = lax.axis_size("y") * lax.axis_size("zh") * lax.axis_size("core")
    total_taps = tap_dev * n_tm
    window_len = driven_wave.shape[0] * n_tm - total_taps
    me = tm_index()
    first_tap = me * tap_dev
    base = total_taps - first_tap - tap_dev
    own, halo_of, edges = split_windows(driven_wave, base, window_len + tap_dev, tap_dev, half_width)
    marks = tap_marks(tap_counts, panel_links, first_tap, tap_dev)
    ports = group_ports
    partial = conv_part(own, responses, marks, window_len, ((half_width, half_width + ports, 1, 0),))
    other_edges = swap_core(edges)
    partial, edges, other_edges = lax.optimization_barrier((partial, edges, other_edges))
    partial = conv_part(
        halo_of(edges, other_edges),
        responses,
        marks,
        window_len,
        ((0, half_width, 0, 0), (half_width + ports, 2 * ports, 2, half_width)),
        partial,
    )
    summed = reduce_scatter(partial, n_tm)
    return summed.astype(jnp.bfloat16)


def solution(mesh):
    band, tm = mesh.devices.shape
    view = Mesh(mesh.devices.reshape(band, tm // 8, 4, 2), ("band",) + TM)
    return jax.shard_map(
        per_device,
        mesh=view,
        in_specs=(P(TM, "band"), P(TM, None, "band"), P("band"), P("band", None)),
        out_specs=P(TM, "band"),
        check_vma=False,
    )
```
